512 devices in a mesh: wide: 64 (over x, z_hi, y), grp: 8 (over z_lo, core).
Axes of the slice: x: 4, y: 4, z: 16 (z_hi: 4, z_lo: 4; z = z_hi * 4 + z_lo), core: 2. Of those that a mesh axis runs over, the one named last changes fastest.
Arguments:
- measured: float32 [512, 64, 2048], P(('wide', 'grp')), may hold values from -768 to 768
- drift: int32 [512], replicated, may hold values from -4 to 4
- start_volume: float32 [64, 32, 2048], P('wide', 'grp'), may hold values from -6 to 6
Outputs:
- estimate: float32 [64, 32, 2048], P('wide', 'grp')
The draws below stay inside these ranges and needn't reach their ends.
All inputs are finite; a program needn't handle non-finite values.
Results may differ from the reference program's by a relative error of at most 0.0001.
Values sent between devices are 32-bit elements; how exact they have to be, the bound alone decides.
A program may use at most 128 MiB of HBM per device.

```python
import math
from functools import reduce
import jax
import jax.numpy as jnp
from jax import lax

A = 512
C = 2048
ITERS = 2
DMAX = 4
Z = 64
NR = 32
MAX_BIN_SHIFT = 22


def touch_ends(entries, stream_key, low, top_value):
    index_at = [jax.random.randint(jax.random.fold_in(stream_key, axis), (), 0, length) for axis, length in enumerate(entries.shape)]
    longest = entries.shape.index(max(entries.shape))
    beside = index_at[:longest] + [(index_at[longest] + 1) % entries.shape[longest]] + index_at[longest + 1:]
    return entries.at[tuple(index_at)].set(low).at[tuple(beside)].set(top_value)


def levels(stream_key, shape, shards, least, largest):
    gain, own = 1.0, jax.random.fold_in(stream_key, 6)
    for dim, blocks in shards:
        steps = jnp.exp(jax.random.uniform(jax.random.fold_in(own, dim), (blocks,), jnp.float32, least / len(shards), largest / len(shards)))
        gain = gain * jnp.repeat(steps, shape[dim] // blocks).reshape([-1 if axis == dim else 1 for axis in range(len(shape))])
    return gain


def noise(rng, dims, width, reach, split=(), kind=jnp.bfloat16):
    drawn = width * jax.random.normal(rng, dims, jnp.float32)
    if split:
        drawn = drawn * levels(rng, dims, split, -0.22, 0.18)
    return jnp.clip(drawn, -reach, reach).astype(kind)


def setup_inputs(seed: int = 0) -> dict:
    key_list = jax.random.split(jax.random.key(seed), 4)
    measured = noise(key_list[0], (A, Z, C), (4 * NR), 768.0, ((0, 512),), jnp.float32)
    drift = touch_ends(jax.random.randint(key_list[1], (A,), 0 - DMAX, DMAX + 1), jax.random.fold_in(key_list[1], 1), 0 - DMAX, DMAX).astype(jnp.int32)
    start_volume = noise(key_list[2], (Z, NR, C), 1.0, 6.0, ((0, 64), (1, 8)), jnp.float32)
    return dict(measured=measured, drift=drift, start_volume=start_volume)


TILT_MAX = math.pi / 4
SMOOTH_EPS = 0.05
TV_STEP = 0.1

def geometry(angle_ids, drift_vals, total_angles, rows, band_extent):
    angle_rad = TILT_MAX * (2.0 * angle_ids.astype(jnp.float32) / (total_angles - 1) - 1.0)
    secant = 1.0 / jnp.cos(angle_rad)
    height = jnp.arange(rows, dtype=jnp.float32) - (rows - 1) / 2.0
    offsets = jnp.arange(2 * band_extent + 1, dtype=jnp.float32) - band_extent
    shifts = height[None, :] * jnp.tan(angle_rad)[:, None] - drift_vals.astype(jnp.float32)[:, None]
    weight_factors = secant[:, None, None] * jnp.maximum(0.0, 1.0 - jnp.abs(shifts[:, :, None] - offsets[None, None, :]))
    return (weight_factors, jnp.cos(angle_rad) / rows)

def secant_sum(total_angles):
    angle_rad = TILT_MAX * (2.0 * jnp.arange(total_angles, dtype=jnp.float32) / (total_angles - 1) - 1.0)
    return jnp.sum(1.0 / jnp.cos(angle_rad))

def apply_correction(row_band_strip, measurement_part, weight_factors, residual_scale, global_scale, band_extent):
    col_count = row_band_strip.shape[2]
    span = 2 * band_extent + 1
    padded = jnp.pad(row_band_strip, ((0, 0), (0, 0), (band_extent, band_extent)))
    shifted = jnp.stack([padded[:, :, shift_id:shift_id + col_count] for shift_id in range(span)], axis=2)
    forward_projected = jnp.einsum('ark,zrku->azu', weight_factors, shifted, precision=lax.Precision.HIGHEST)
    residual_error = residual_scale[:, None, None] * (measurement_part - forward_projected)
    spread = jnp.einsum('ark,azu->kzru', weight_factors, residual_error, precision=lax.Precision.HIGHEST)
    spread = jnp.pad(spread, ((0, 0), (0, 0), (0, 0), (band_extent, band_extent)))
    pieces = [spread[shift_id, :, :, 2 * band_extent - shift_id:2 * band_extent - shift_id + col_count] for shift_id in range(span)]
    return global_scale * reduce(lambda left, right: left + right, pieces)

def divergence(extended, z_first, r_first, zcount, rcount):
    plane_count, height, col_count = extended.shape
    z_index = z_first + jnp.arange(plane_count, dtype=jnp.int32)[:, None, None]
    row_index = r_first + jnp.arange(height, dtype=jnp.int32)[None, :, None]
    col_index = jnp.arange(col_count, dtype=jnp.int32)[None, None, :]
    diff_z = jnp.concatenate([extended[1:] - extended[:-1], jnp.zeros_like(extended[:1])], axis=0)
    diff_z = jnp.where((z_index >= 0) & (z_index < zcount - 1), diff_z, 0.0)
    diff_r = jnp.concatenate([extended[:, 1:] - extended[:, :-1], jnp.zeros_like(extended[:, :1])], axis=1)
    diff_r = jnp.where((row_index >= 0) & (row_index < rcount - 1), diff_r, 0.0)
    diff_c = jnp.concatenate([extended[:, :, 1:] - extended[:, :, :-1], jnp.zeros_like(extended[:, :, :1])], axis=2)
    diff_c = jnp.where(col_index < col_count - 1, diff_c, 0.0)
    magnitude = jnp.sqrt(diff_z * diff_z + diff_r * diff_r + diff_c * diff_c + SMOOTH_EPS * SMOOTH_EPS)
    unit_z = diff_z / magnitude
    unit_r = diff_r / magnitude
    unit_c = diff_c / magnitude
    back_c = unit_c - jnp.concatenate([jnp.zeros_like(unit_c[:, :, :1]), unit_c[:, :, :-1]], axis=2)
    return unit_z[1:-1, 1:-1] - unit_z[:-2, 1:-1] + (unit_r[1:-1, 1:-1] - unit_r[1:-1, :-2]) + back_c[1:-1, 1:-1]

def reference(measured, drift, start_volume):
    angle_ids = jnp.arange(A, dtype=jnp.int32)
    weight_factors, residual_scale = geometry(angle_ids, drift, A, NR, MAX_BIN_SHIFT)
    global_scale = 1.0 / secant_sum(A)
    sinograms = jnp.moveaxis(measured, 1, 0)
    volume = start_volume
    for sweep in range(ITERS):

        def per_slice(packed_stack):
            rows_of_slice, slice_measurement = packed_stack
            return apply_correction(rows_of_slice[None], slice_measurement[:, None, :], weight_factors, residual_scale, global_scale, MAX_BIN_SHIFT)[0]
        volume = volume + lax.map(per_slice, (volume, sinograms))
        extended = jnp.pad(volume, ((1, 1), (1, 1), (0, 0)))
        volume = volume + TV_STEP * divergence(extended, -1, -1, Z, NR)
    return volume
```

```python
import functools
import math

import jax
import jax.numpy as jnp
import ml_dtypes
import numpy as np
from jax import lax
from jax.experimental import pallas as pl
from jax.experimental.pallas import tpu as pltpu
from jax.sharding import PartitionSpec as P

MESH = pl.DeviceIdType.MESH
A = 512
C = 2048
Z = 64
NR = 32
DMAX = 4
EPS = 0.05
TV_STEP = 0.1
KB = 20
NK = 2 * KB + 1
KD = 16
NKD = 2 * KD + 1
NKP = 36
JT = 32
NJ = 2 * JT + 1
PAD = 64
WIN = 384
OWN = 256
WIDE = 128 + C + 128
F32 = jnp.float32
BF16 = jnp.bfloat16


def tables():
    angle = (math.pi / 4) * (2.0 * np.arange(A) / (A - 1) - 1.0)
    tan, sec = np.tan(angle), 1.0 / np.cos(angle)
    scale = 1.0 / sec.sum() / NR
    height = np.arange(NR) - (NR - 1) / 2.0
    offsets = np.arange(-KD, KD + 1)
    tri = np.maximum(0.0, 1.0 - np.abs(height[None, :, None] * tan[:, None, None] - offsets))
    t = np.zeros((NJ, NR, NR))
    for n, j in enumerate(range(-JT, JT + 1)):
        lo, hi = max(-KD, -KD - j), min(KD, KD - j)
        if lo <= hi:
            k = np.arange(lo, hi + 1) + KD
            left = np.transpose(tri[:, :, k] * sec[:, None, None], (1, 0, 2)).reshape(NR, -1)
            right = np.transpose(tri[:, :, k + j], (1, 0, 2)).reshape(NR, -1)
            t[n] = left @ right.T
    t *= scale

    def split(x):
        x = x.astype(np.float32)
        hi = x.astype(ml_dtypes.bfloat16)
        return hi, (x - hi.astype(np.float32)).astype(ml_dtypes.bfloat16)

    t_hi, t_lo = split(t.reshape(NJ * NR, NR))
    t4 = np.concatenate([t_hi, t_hi, t_lo, t_lo], axis=1)
    kr = np.transpose(tri, (0, 2, 1)).reshape(A, NKD * NR)
    front = np.zeros((A, NKP * NR))
    front[:, : NKD * NR] = kr * sec[:, None]
    f_hi, f_lo = split(front)
    b_hi, b_lo = split(kr.T * scale)
    slots = np.zeros((8, 64))
    for zh in range(4):
        for c in range(2):
            for s in range(64):
                x, zl, y = s // 16, (s // 4) % 4, s % 4
                slots[zh * 2 + c, s] = tan[(x * 16 + zh * 4 + y) * 8 + zl * 2 + c]
    slots = np.tile(slots, (1, 4)).astype(np.float32)
    return scale, slots, t4, f_hi, f_lo, b_hi, b_lo


def halves(x):
    hi = x.astype(BF16)
    return hi, (x - hi.astype(F32)).astype(BF16)


def place():
    wide, grp = lax.axis_index("wide"), lax.axis_index("grp")
    return wide // 16, (wide // 4) % 4, wide % 4, grp // 2, grp % 2


def device(x, zh, y, zl, c):
    return {"wide": x * 16 + zh * 4 + y, "grp": zl * 2 + c}


def lane(shape):
    return lax.broadcasted_iota(jnp.int32, shape, len(shape) - 1)


def sub(shape):
    return lax.broadcasted_iota(jnp.int32, shape, 0)


def tv_rows(mid, up, down, z, row0):
    shape = mid.shape
    row = row0 - 1 + sub(shape)
    inside = (row >= 0) & (row < NR - 1)
    last = lane(shape) < C - 1

    def units(centre, above):
        dr = jnp.where(inside, pltpu.roll(centre, 7, 0) - centre, 0.0)
        dc = jnp.where(last, pltpu.roll(centre, C - 1, 1) - centre, 0.0)
        inv = lax.rsqrt(above * above + dr * dr + dc * dc + EPS * EPS)
        return dr, dc, inv

    dz = jnp.where(z < Z - 1, up - mid, 0.0)
    dr, dc, inv = units(mid, dz)
    uz, ur, uc = dz * inv, dr * inv, dc * inv
    dz_b = jnp.where(z > 0, mid - down, 0.0)
    _, _, inv_b = units(down, dz_b)
    uc_b = jnp.where(lane(shape) > 0, pltpu.roll(uc, 1, 1), 0.0)
    return uz - dz_b * inv_b + (ur - pltpu.roll(ur, 1, 0)) + (uc - uc_b)


def kernel(
    scale,
    meas, drift, v0, slots, t4_h, fh_h, fl_h, bh_h, bl_h,
    out,
    t4, fh, fl, bh, bl, buf, spare, wts, xb, big,
    psend, precv, rsend, rrecv,
    vpad, win, rhs, gt, im, dcol, basis, cols, brow, bwin,
    hbox, hz, hrow, blk, cmb,
    csem, asem_s, asem_r, psem, rsem_s, rsem_r, wsem_s, wsem_r, qsem_s, qsem_r, bsem_s, bsem_r, hsem_s, hsem_r, msem_s, msem_r,
):
    wide, grp = lax.axis_index("wide"), lax.axis_index("grp")
    x, zh, y, zl, c = place()

    loads = [
        pltpu.make_async_copy(src, dst, csem.at[n])
        for n, (src, dst) in enumerate(
            ((fh_h, fh), (fl_h, fl), (bh_h, bh), (bl_h, bl), (t4_h, t4))
        )
    ]
    for load in loads:
        load.start()

    def block_peer(i):
        px, pl_, py = x ^ (i // 16), zl ^ ((i // 4) % 4), y ^ (i % 4)
        return device(px, zh, py, pl_, c), px * 16 + pl_ * 4 + py

    slices = [{"wide": (wide + d + Z) % Z, "grp": g} for d in (-1, 1) for g in range(8)]
    others = [device(x, zh, y, q, 1 - c) for q in range(4)]
    ring = [device(x, zh ^ i, y, q, c) for i in range(1, 4) for q in range(4)]

    barrier = pltpu.get_barrier_semaphore()

    def greet(i, carry):
        pl.semaphore_signal(barrier, inc=1, device_id=block_peer(i)[0], device_id_type=MESH)
        return carry

    lax.fori_loop(1, 64, greet, 0)
    for who in others + ring + slices:
        pl.semaphore_signal(barrier, inc=1, device_id=who, device_id_type=MESH)

    def pad_columns(rows):
        vpad[...] = pltpu.roll(
            jnp.concatenate([rows, jnp.zeros((4, 128), F32)], axis=1), PAD, 1
        )

    pad_columns(v0[0])
    pl.semaphore_wait(barrier, 63 + len(others) + len(ring) + len(slices))

    me_slot = x * 16 + zl * 4 + y

    def give(i, carry):
        who, slot = block_peer(i)
        pltpu.make_async_remote_copy(
            src_ref=meas.at[0, slot],
            dst_ref=buf.at[me_slot],
            send_sem=asem_s,
            recv_sem=asem_r,
            device_id=who,
            device_id_type=MESH,
        ).start()
        return carry

    def spread(sem_s, sem_r, source, target):
        pltpu.make_async_copy(source(grp), target(grp), sem_r.at[grp]).start()
        copies = []
        for i in range(1, 8):
            peer = grp ^ i
            copy = pltpu.make_async_remote_copy(
                src_ref=source(peer),
                dst_ref=target(grp),
                send_sem=sem_s.at[i],
                recv_sem=sem_r.at[grp],
                device_id={"grp": peer},
                device_id_type=MESH,
            )
            copy.start()
            copies.append(copy)
        return copies

    def arrived(sem_r, target):
        for g in range(8):
            pltpu.make_async_copy(target(g), target(g), sem_r.at[g]).wait()

    def window(g):
        return vpad.at[:, pl.ds(pl.multiple_of(g * OWN, OWN), WIN)]

    def own_columns(ref, g):
        return ref.at[:, pl.ds(pl.multiple_of(g * OWN, OWN), OWN)]

    sent_w0 = spread(wsem_s.at[0], wsem_r.at[0], window, lambda g: win.at[0, g])
    lax.fori_loop(1, 64, give, 0)
    pltpu.make_async_copy(meas.at[0, me_slot], buf.at[me_slot], asem_r).start()
    pltpu.make_async_copy(meas.at[0, me_slot], spare.at[0], asem_s).start()

    for q in range(4):
        eye = sub((128, 128)) == lane((128, 128))
        line = jnp.broadcast_to(drift[q : q + 1, :].astype(F32), (128, 128))
        dcol[q * 128 : (q + 1) * 128, :] = jnp.broadcast_to(
            jnp.sum(jnp.where(eye, line, 0.0), axis=1, keepdims=True), (128, 128)
        )
    s = lane((8, 128)) % 64
    view = ((s // 16) * 16 + zh * 4 + s % 4) * 8 + ((s // 4) % 4) * 2 + c

    total = jnp.zeros((8, 128), F32)
    view_b = jnp.broadcast_to(view[0:1, :], (128, 128))
    for q in range(4):
        hit = view_b == (q * 128 + sub((128, 128)))
        total = total + jnp.sum(
            jnp.where(hit, dcol[q * 128 : (q + 1) * 128, :], 0.0), axis=0, keepdims=True
        )
    shift_d = jnp.concatenate([total[0:1], total[0:1]], axis=1)
    tan = slots[pl.ds(zh * 2 + c, 1), :]

    def weigh(n, carry):
        rel, k = n // NK, n % NK
        core = jnp.where(rel == 0, 1 - c, c)
        t = sub((16, 256))
        r = (t // 4) * 8 + core * 4 + t % 4
        height = r.astype(F32) - (NR - 1) / 2.0
        w = (
            jnp.maximum(0.0, 1.0 - jnp.abs(height * tan - shift_d - (k - KB).astype(F32))) * scale
        )
        hi = w.astype(BF16)
        lo = (w - hi.astype(F32)).astype(BF16)
        wts[pl.ds(pl.multiple_of(n * 16, 16), 16), :] = jnp.where(
            lane((16, 256)) < 128, hi.astype(F32), lo.astype(F32)
        ).astype(BF16)
        return carry

    lax.fori_loop(0, 2 * NK, weigh, 0)
    xb[:, 0:128] = jnp.zeros((256, 128), BF16)
    xb[:, WIDE - 128 :] = jnp.zeros((256, 128), BF16)
    im[...] = jnp.zeros_like(im)

    for load in loads:
        load.wait()

    def project(slot):
        v = jnp.concatenate([win[slot, g] for g in range(8)], axis=0)
        hi, lo = halves(v)
        rhs[0:32], rhs[32:64], rhs[64:96], rhs[96:128] = hi, lo, hi, lo
        gt[...] = jnp.dot(t4[...], rhs[...], preferred_element_type=F32)
        acc = jnp.zeros((NR, OWN), F32)
        for n in range(NJ):
            g = gt[n * NR : (n + 1) * NR, :]
            acc = acc + pltpu.roll(g, WIN - (PAD + n - JT), 1)[:, :OWN]
        for n in range(NKD):
            k = n - KD
            left = pltpu.roll(v, WIN - (48 + k), 1)[:, :128]
            right = pltpu.roll(v, WIN - (252 + k), 1)[:, :128]
            e = jnp.where(lane((NR, 128)) < 64, left, right)
            e_hi, e_lo = halves(e)
            im[n * NR : (n + 1) * NR, 0:128] = e_hi
            im[n * NR : (n + 1) * NR, 128:256] = e_lo
        p2 = jnp.dot(fh[...], im[...], preferred_element_type=F32)
        p = p2[:, :128] + p2[:, 128:] + jnp.dot(fl[...], im[:, 0:128], preferred_element_type=F32)
        pos = lane((A, 128))
        d = dcol[...]
        at = pos.astype(F32)
        cut_l = (grp == 0) & (pos < 20) & (at - 16.0 < -d)
        cut_r = (grp == 7) & (pos >= 64) & (pos < 84) & (at - 64.0 > 3.0 - d)
        p = jnp.where(cut_l | cut_r, p, 0.0)
        p_hi, p_lo = halves(p)
        basis[:, 0:128] = p_hi
        basis[:, 128:256] = p_lo
        g2 = jnp.dot(bh[...], basis[...], preferred_element_type=F32)
        g2 = g2[:, :128] + g2[:, 128:]
        g2 = g2 + jnp.dot(bl[...], basis[:, 0:128], preferred_element_type=F32)
        e = jnp.zeros((NR, 128), F32)
        for n in range(NKD):
            e = e + pltpu.roll(g2[n * NR : (n + 1) * NR, :], (n - KD - 16) % 128, 1)
        pos = lane((NR, 128))
        e_l = jnp.where(pos < 20, e, 0.0)
        e_r = jnp.where(pos >= 108, pltpu.roll(e, 76, 1), 0.0)
        return acc - jnp.concatenate([e_l, e_r], axis=1), pltpu.roll(v, WIN - PAD, 1)[:, :OWN]

    arrived(wsem_r.at[0], lambda g: win.at[0, g])
    q0, own0 = project(0)
    base = own0 - q0
    for g in range(8):
        cols[g] = base[4 * g : 4 * g + 4, :]
    sent_q = spread(
        qsem_s, qsem_r, lambda g: cols.at[g], lambda g: own_columns(brow.at[0], g)
    )

    pltpu.make_async_copy(buf, buf, asem_r).wait()
    for q in range(2):
        cut = slice(q * 1024, (q + 1) * 1024)
        to = slice(128 + q * 1024, 128 + (q + 1) * 1024)
        hi, lo = halves(buf[:, cut])
        xb[0:64, to], xb[64:128, to], xb[128:192, to], xb[192:256, to] = hi, lo, hi, lo

    def partial_rows(rel):
        w = wts[rel * NK * 16 : (rel + 1) * NK * 16, :]
        for t in range(WIDE // 256):
            big[:, t * 256 : (t + 1) * 256] = jnp.dot(
                w, xb[:, t * 256 : (t + 1) * 256], preferred_element_type=F32
            )
        tiles = []
        for half in range(2):
            acc = jnp.zeros((8, C), F32)
            for k in range(NK):
                g = big[k * 16 + half * 8 : k * 16 + half * 8 + 8, :]
                acc = acc + pltpu.roll(g, (k - KB) % WIDE, 1)[:, 128 : 128 + C]
            tiles.append(acc)
        return tiles

    tiles = partial_rows(0)
    psend[0], psend[1] = tiles[0], tiles[1]
    pair = pltpu.make_async_remote_copy(
        src_ref=psend,
        dst_ref=precv,
        send_sem=psem.at[0],
        recv_sem=psem.at[1],
        device_id={"grp": grp ^ 1},
        device_id_type=MESH,
    )
    pair.start()
    tiles = partial_rows(1)
    pair.wait_recv()
    for half in range(2):
        both = tiles[half] + precv[half]
        rsend[2 * half] = both[0:4]
        rsend[2 * half + 1] = both[4:8]
    for q in range(4):
        mine = (zh == zl) & (zl == q)

        @pl.when(mine)
        def _():
            pltpu.make_async_copy(rsend.at[q], rrecv.at[zh], rsem_r.at[zh]).start()

        @pl.when(jnp.logical_not(mine))
        def _():
            pltpu.make_async_remote_copy(
                src_ref=rsend.at[q],
                dst_ref=rrecv.at[zh],
                send_sem=rsem_s.at[q],
                recv_sem=rsem_r.at[zh],
                device_id=device(x, zl, y, q, c),
                device_id_type=MESH,
            ).start()

    arrived(qsem_r, lambda g: own_columns(brow.at[0], g))
    for q in range(4):
        pltpu.make_async_copy(rrecv.at[q], rrecv.at[q], rsem_r.at[q]).wait()
    b = (rrecv[0] + rrecv[1]) + (rrecv[2] + rrecv[3])
    brow[1] = b
    half1 = brow[0] + b
    hbox[...] = half1

    up_w, down_w = (wide + 1) % Z, (wide + Z - 1) % Z
    next_g, last_g = (grp + 1) % 8, (grp + 7) % 8
    moves = [
        (hbox, hz.at[0], {"wide": down_w}),
        (hbox, hz.at[1], {"wide": up_w}),
        (hbox.at[3], hrow.at[0], {"grp": next_g}),
        (hbox.at[0], hrow.at[1], {"grp": last_g}),
        (hbox.at[3], hrow.at[2], {"wide": down_w, "grp": next_g}),
        (hbox.at[0], hrow.at[3], {"wide": up_w, "grp": last_g}),
    ]
    sent_h = []
    for n, (src, dst, who) in enumerate(moves):
        copy = pltpu.make_async_remote_copy(
            src_ref=src,
            dst_ref=dst,
            send_sem=hsem_s.at[n],
            recv_sem=hsem_r.at[n],
            device_id=who,
            device_id_type=MESH,
        )
        copy.start()
        sent_h.append(copy)
    sent_b = spread(bsem_s, bsem_r, lambda g: own_columns(brow.at[1], g), lambda g: bwin.at[g])
    for copy in sent_w0:
        copy.wait_send()
    for copy in sent_h:
        copy.wait_recv()

    def eight(rows):
        return jnp.concatenate([rows[0:1], rows, jnp.zeros((3, C), F32)], axis=0)

    at = sub((8, C))
    mid = jnp.where(at == 0, hrow[0:1], jnp.where(at == 5, hrow[1:2], eight(half1)))
    up = jnp.where(at == 0, hrow[2:3], eight(hz[0]))
    down = jnp.where(at == 5, hrow[3:4], eight(hz[1]))
    v1 = mid + TV_STEP * tv_rows(mid, up, down, wide, 4 * grp)
    pad_columns(v1[1:5])

    sent_w1 = spread(wsem_s.at[1], wsem_r.at[1], window, lambda g: win.at[1, g])
    arrived(bsem_r, lambda g: bwin.at[g])
    arrived(wsem_r.at[1], lambda g: win.at[1, g])
    q1, own1 = project(1)
    half2 = own1 - q1 + jnp.concatenate([bwin[g] for g in range(8)], axis=0)
    edge = jnp.zeros((1, OWN), F32)
    for g in range(8):
        before = half2[4 * g - 1 : 4 * g] if g else edge
        after = half2[4 * g + 4 : 4 * g + 5] if g < 7 else edge
        blk[g] = jnp.concatenate([before, half2[4 * g : 4 * g + 4], after, edge, edge], axis=0)

    sent_m = []
    for d in range(3):
        to = (wide + (0, Z - 1, 1)[d]) % Z
        for i in range(8):
            peer = grp ^ i
            dst = cmb.at[d, :, pl.ds(pl.multiple_of(grp * OWN, OWN), OWN)]
            if d == 0 and i == 0:
                pltpu.make_async_copy(blk.at[grp], dst, msem_r.at[0, grp]).start()
                continue
            copy = pltpu.make_async_remote_copy(
                src_ref=blk.at[peer],
                dst_ref=dst,
                send_sem=msem_s.at[d, i],
                recv_sem=msem_r.at[d, grp],
                device_id={"wide": to, "grp": peer},
                device_id_type=MESH,
            )
            copy.start()
            sent_m.append(copy)
    for copies in (sent_q, [pair], sent_h, sent_b, sent_w1):
        for copy in copies:
            copy.wait_send()
    for q in range(4):

        @pl.when(jnp.logical_not((zh == zl) & (zl == q)))
        def _():
            pltpu.make_async_copy(rsend.at[q], rsend.at[q], rsem_s.at[q]).wait()

    pltpu.make_async_copy(buf, buf, asem_s).wait()
    for d in range(3):
        for g in range(8):
            part = cmb.at[d, :, pl.ds(g * OWN, OWN)]
            pltpu.make_async_copy(part, part, msem_r.at[d, g]).wait()
    v2 = cmb[0] + TV_STEP * tv_rows(cmb[0], cmb[1], cmb[2], wide, 4 * grp)
    out[0] = v2[1:5]
    for copy in sent_m:
        copy.wait_send()


def on_device(measured, drift, start_volume):
    scale, slots, t4, f_hi, f_lo, b_hi, b_lo = tables()
    vmem = pl.BlockSpec(memory_space=pltpu.VMEM)
    hbm = pl.BlockSpec(memory_space=pltpu.HBM)
    dma = pltpu.SemaphoreType.DMA
    scratch = [
        pltpu.VMEM(t4.shape, BF16),
        pltpu.VMEM(f_hi.shape, BF16),
        pltpu.VMEM(f_lo.shape, BF16),
        pltpu.VMEM(b_hi.shape, BF16),
        pltpu.VMEM(b_lo.shape, BF16),
        pltpu.VMEM((64, C), F32),
        pltpu.VMEM((8, C), F32),
        pltpu.VMEM((2 * NK * 16, 256), BF16),
        pltpu.VMEM((256, WIDE), BF16),
        pltpu.VMEM((NK * 16, WIDE), F32),
        pltpu.VMEM((2, 8, C), F32),
        pltpu.VMEM((2, 8, C), F32),
        pltpu.VMEM((4, 4, C), F32),
        pltpu.VMEM((4, 4, C), F32),
        pltpu.VMEM((4, C + 128), F32),
        pltpu.VMEM((2, 8, 4, WIN), F32),
        pltpu.VMEM((128, WIN), BF16),
        pltpu.VMEM((NJ * NR, WIN), F32),
        pltpu.VMEM((NKP * NR, 256), BF16),
        pltpu.VMEM((A, 128), F32),
        pltpu.VMEM((A, 256), BF16),
        pltpu.VMEM((8, 4, OWN), F32),
        pltpu.VMEM((2, 4, C), F32),
        pltpu.VMEM((8, 4, OWN), F32),
        pltpu.VMEM((4, C), F32),
        pltpu.VMEM((2, 4, C), F32),
        pltpu.VMEM((4, C), F32),
        pltpu.VMEM((8, 8, OWN), F32),
        pltpu.VMEM((3, 8, C), F32),
        dma((5,)),
        dma,
        dma,
        dma((2,)),
        dma((4,)),
        dma((4,)),
        dma((2, 8)),
        dma((2, 8)),
        dma((8,)),
        dma((8,)),
        dma((8,)),
        dma((8,)),
        dma((6,)),
        dma((6,)),
        dma((3, 8)),
        dma((3, 8)),
    ]
    return pl.pallas_call(
        functools.partial(kernel, float(scale)),
        out_shape=jax.ShapeDtypeStruct(start_volume.shape, F32),
        in_specs=[hbm, vmem, vmem, vmem] + [hbm] * 5,
        out_specs=vmem,
        scratch_shapes=scratch,
        compiler_params=pltpu.CompilerParams(
            collective_id=0, has_side_effects=True, vmem_limit_bytes=2**26 - 2**18
        ),
        name="sirt",
    )(
        measured,
        drift.reshape(4, 128),
        start_volume,
        jnp.asarray(slots),
        *(jnp.asarray(t) for t in (t4, f_hi, f_lo, b_hi, b_lo)),
    )


def solution(mesh):
    in_specs = (P(("wide", "grp"), None, None), P(), P("wide", "grp", None))
    return jax.shard_map(
        on_device, mesh=mesh, in_specs=in_specs, out_specs=P("wide", "grp", None), check_vma=False
    )
```

```python
import functools
import math

import jax
import jax.numpy as jnp
import ml_dtypes
import numpy as np
from jax import lax
from jax.experimental import pallas as pl
from jax.experimental.pallas import tpu as pltpu
from jax.sharding import PartitionSpec as P

MESH = pl.DeviceIdType.MESH
A = 512
C = 2048
Z = 64
NR = 32
DMAX = 4
EPS = 0.05
TV_STEP = 0.1
KB = 20
NK = 2 * KB + 1
KD = 16
NKD = 2 * KD + 1
NKP = 36
JT = 32
NJ = 2 * JT + 1
PAD = 64
WIN = 384
OWN = 256
WIDE = 128 + C + 128
F32 = jnp.float32
BF16 = jnp.bfloat16


def tables():
    angle = (math.pi / 4) * (2.0 * np.arange(A) / (A - 1) - 1.0)
    tan, sec = np.tan(angle), 1.0 / np.cos(angle)
    scale = 1.0 / sec.sum() / NR
    height = np.arange(NR) - (NR - 1) / 2.0
    offsets = np.arange(-KD, KD + 1)
    tri = np.maximum(0.0, 1.0 - np.abs(height[None, :, None] * tan[:, None, None] - offsets))
    t = np.zeros((NJ, NR, NR))
    for n, j in enumerate(range(-JT, JT + 1)):
        lo, hi = max(-KD, -KD - j), min(KD, KD - j)
        if lo <= hi:
            k = np.arange(lo, hi + 1) + KD
            left = np.transpose(tri[:, :, k] * sec[:, None, None], (1, 0, 2)).reshape(NR, -1)
            right = np.transpose(tri[:, :, k + j], (1, 0, 2)).reshape(NR, -1)
            t[n] = left @ right.T
    t *= scale

    def split(x):
        x = x.astype(np.float32)
        hi = x.astype(ml_dtypes.bfloat16)
        return hi, (x - hi.astype(np.float32)).astype(ml_dtypes.bfloat16)

    t_hi, t_lo = split(t.reshape(NJ * NR, NR))
    t4 = np.concatenate([t_hi, t_hi, t_lo, t_lo], axis=1)
    kr = np.transpose(tri, (0, 2, 1)).reshape(A, NKD * NR)
    front = np.zeros((A, NKP * NR))
    front[:, : NKD * NR] = kr * sec[:, None]
    f_hi, f_lo = split(front)
    b_hi, b_lo = split(kr.T * scale)
    slots = np.zeros((8, 64))
    for zh in range(4):
        for c in range(2):
            for s in range(64):
                x, zl, y = s // 16, (s // 4) % 4, s % 4
                slots[zh * 2 + c, s] = tan[(x * 16 + zh * 4 + y) * 8 + zl * 2 + c]
    slots = np.tile(slots, (1, 4)).astype(np.float32)
    return scale, slots, t4, f_hi, f_lo, b_hi, b_lo


def halves(x):
    hi = x.astype(BF16)
    return hi, (x - hi.astype(F32)).astype(BF16)


def place():
    wide, grp = lax.axis_index("wide"), lax.axis_index("grp")
    return wide // 16, (wide // 4) % 4, wide % 4, grp // 2, grp % 2


def device(x, zh, y, zl, c):
    return {"wide": x * 16 + zh * 4 + y, "grp": zl * 2 + c}


def lane(shape):
    return lax.broadcasted_iota(jnp.int32, shape, len(shape) - 1)


def sub(shape):
    return lax.broadcasted_iota(jnp.int32, shape, 0)


def tv_rows(mid, up, down, z, row0):
    shape = mid.shape
    row = row0 - 1 + sub(shape)
    inside = (row >= 0) & (row < NR - 1)
    last = lane(shape) < C - 1

    def units(centre, above):
        dr = jnp.where(inside, pltpu.roll(centre, 7, 0) - centre, 0.0)
        dc = jnp.where(last, pltpu.roll(centre, C - 1, 1) - centre, 0.0)
        inv = lax.rsqrt(above * above + dr * dr + dc * dc + EPS * EPS)
        return dr, dc, inv

    dz = jnp.where(z < Z - 1, up - mid, 0.0)
    dr, dc, inv = units(mid, dz)
    uz, ur, uc = dz * inv, dr * inv, dc * inv
    dz_b = jnp.where(z > 0, mid - down, 0.0)
    _, _, inv_b = units(down, dz_b)
    uc_b = jnp.where(lane(shape) > 0, pltpu.roll(uc, 1, 1), 0.0)
    return uz - dz_b * inv_b + (ur - pltpu.roll(ur, 1, 0)) + (uc - uc_b)


def kernel(
    scale,
    meas, drift, v0, slots, t4_h, fh_h, fl_h, bh_h, bl_h,
    out,
    t4, fh, fl, bh, bl, buf, spare, wts, xb, big,
    psend, precv, rsend, rrecv,
    vpad, win, rhs, gt, im, dcol, basis, cols, brow,
    hbox, hz, hrow,
    csem, asem_s, asem_r, psem_s, psem_r, rsem_s, rsem_r, wsem_s, wsem_r, qsem_s, qsem_r, hsem_s, hsem_r,
):
    wide, grp = lax.axis_index("wide"), lax.axis_index("grp")
    x, zh, y, zl, c = place()
    up_w, down_w = (wide + 1) % Z, (wide + Z - 1) % Z
    next_g, last_g = (grp + 1) % 8, (grp + 7) % 8

    def block_peer(i):
        px, pl_, py = x ^ ((i // 4) % 4), zl ^ (3 - i // 16), y ^ (i % 4)
        return device(px, zh, py, pl_, c), px * 16 + pl_ * 4 + py

    barrier = pltpu.get_barrier_semaphore()

    def hello(who):
        pl.semaphore_signal(barrier, inc=1, device_id=who, device_id_type=MESH)

    def greet(i, carry):
        hello(block_peer(i)[0])
        return carry

    away = zh != zl
    for who in (
        {"wide": up_w},
        {"wide": down_w},
        {"wide": down_w, "grp": next_g},
        {"wide": up_w, "grp": last_g},
    ):
        hello(who)
    for i in range(1, 4):
        hello(device(x, zh ^ i, y, zh, c))

    @pl.when(away)
    def _():
        for q in range(4):
            hello(device(x, zl, y, q, c))

    lax.fori_loop(0, 48, greet, 0)
    lax.fori_loop(49, 64, greet, 0)
    for q in range(4):
        hello(device(x, zh, y, q, 1 - c))

    loads = [
        pltpu.make_async_copy(src, dst, csem.at[n])
        for n, (src, dst) in enumerate(
            ((fh_h, fh), (fl_h, fl), (bh_h, bh), (bl_h, bl), (t4_h, t4))
        )
    ]
    for load in loads:
        load.start()

    def pad_columns(rows):
        vpad[...] = pltpu.roll(
            jnp.concatenate([rows, jnp.zeros((4, 128), F32)], axis=1), PAD, 1
        )

    pad_columns(v0[0])
    pl.semaphore_wait(barrier, 63 + 4 + 3 + 4 + jnp.where(away, 4, 0))

    me_slot = x * 16 + zl * 4 + y

    def give(i, carry):
        who, slot = block_peer(i)
        pltpu.make_async_remote_copy(
            src_ref=meas.at[0, slot],
            dst_ref=buf.at[me_slot],
            send_sem=asem_s,
            recv_sem=asem_r,
            device_id=who,
            device_id_type=MESH,
        ).start()
        return carry

    def spread(sem_s, sem_r, source, target):
        pltpu.make_async_copy(source(grp), target(grp), sem_r.at[grp]).start()
        copies = []
        for i in range(7, 0, -1):
            peer = grp ^ i
            copy = pltpu.make_async_remote_copy(
                src_ref=source(peer),
                dst_ref=target(grp),
                send_sem=sem_s.at[i],
                recv_sem=sem_r.at[grp],
                device_id={"grp": peer},
                device_id_type=MESH,
            )
            copy.start()
            copies.append(copy)
        return copies

    def arrived(sem_r, target):
        for g in range(8):
            pltpu.make_async_copy(target(g), target(g), sem_r.at[g]).wait()

    def window(g):
        return vpad.at[:, pl.ds(pl.multiple_of(g * OWN, OWN), WIN)]

    def own_columns(ref, g):
        return ref.at[:, pl.ds(pl.multiple_of(g * OWN, OWN), OWN)]

    sent_w = spread(wsem_s.at[0], wsem_r.at[0], window, lambda g: win.at[0, g])
    lax.fori_loop(0, 48, give, 0)
    lax.fori_loop(49, 64, give, 0)
    pltpu.make_async_copy(meas.at[0, me_slot], buf.at[me_slot], asem_r).start()
    pltpu.make_async_copy(meas.at[0, me_slot], spare.at[0], asem_s).start()

    for q in range(4):
        eye = sub((128, 128)) == lane((128, 128))
        line = jnp.broadcast_to(drift[q : q + 1, :].astype(F32), (128, 128))
        dcol[q * 128 : (q + 1) * 128, :] = jnp.broadcast_to(
            jnp.sum(jnp.where(eye, line, 0.0), axis=1, keepdims=True), (128, 128)
        )
    s = lane((8, 128)) % 64
    view = ((s // 16) * 16 + zh * 4 + s % 4) * 8 + ((s // 4) % 4) * 2 + c

    total = jnp.zeros((8, 128), F32)
    view_b = jnp.broadcast_to(view[0:1, :], (128, 128))
    for q in range(4):
        hit = view_b == (q * 128 + sub((128, 128)))
        total = total + jnp.sum(
            jnp.where(hit, dcol[q * 128 : (q + 1) * 128, :], 0.0), axis=0, keepdims=True
        )
    shift_d = jnp.concatenate([total[0:1], total[0:1]], axis=1)
    tan = slots[pl.ds(zh * 2 + c, 1), :]

    def weigh(n, carry):
        rel, k = n // NK, n % NK
        core = jnp.where(rel == 0, 1 - c, c)
        t = sub((16, 256))
        r = (t // 4) * 8 + core * 4 + t % 4
        height = r.astype(F32) - (NR - 1) / 2.0
        w = (
            jnp.maximum(0.0, 1.0 - jnp.abs(height * tan - shift_d - (k - KB).astype(F32))) * scale
        )
        hi = w.astype(BF16)
        lo = (w - hi.astype(F32)).astype(BF16)
        wts[pl.ds(pl.multiple_of(n * 16, 16), 16), :] = jnp.where(
            lane((16, 256)) < 128, hi.astype(F32), lo.astype(F32)
        ).astype(BF16)
        return carry

    lax.fori_loop(0, 2 * NK, weigh, 0)
    xb[:, 0:128] = jnp.zeros((256, 128), BF16)
    xb[:, WIDE - 128 :] = jnp.zeros((256, 128), BF16)
    im[...] = jnp.zeros_like(im)

    for load in loads:
        load.wait()

    def project(slot):
        v = jnp.concatenate([win[slot, g] for g in range(8)], axis=0)
        hi, lo = halves(v)
        rhs[0:32], rhs[32:64], rhs[64:96], rhs[96:128] = hi, lo, hi, lo
        gt[...] = jnp.dot(t4[...], rhs[...], preferred_element_type=F32)
        acc = jnp.zeros((NR, OWN), F32)
        for n in range(NJ):
            g = gt[n * NR : (n + 1) * NR, :]
            acc = acc + pltpu.roll(g, WIN - (PAD + n - JT), 1)[:, :OWN]
        for n in range(NKD):
            k = n - KD
            left = pltpu.roll(v, WIN - (48 + k), 1)[:, :128]
            right = pltpu.roll(v, WIN - (252 + k), 1)[:, :128]
            e = jnp.where(lane((NR, 128)) < 64, left, right)
            e_hi, e_lo = halves(e)
            im[n * NR : (n + 1) * NR, 0:128] = e_hi
            im[n * NR : (n + 1) * NR, 128:256] = e_lo
        p2 = jnp.dot(fh[...], im[...], preferred_element_type=F32)
        p = p2[:, :128] + p2[:, 128:] + jnp.dot(fl[...], im[:, 0:128], preferred_element_type=F32)
        pos = lane((A, 128))
        d = dcol[...]
        at = pos.astype(F32)
        cut_l = (grp == 0) & (pos < 20) & (at - 16.0 < -d)
        cut_r = (grp == 7) & (pos >= 64) & (pos < 84) & (at - 64.0 > 3.0 - d)
        p = jnp.where(cut_l | cut_r, p, 0.0)
        p_hi, p_lo = halves(p)
        basis[:, 0:128] = p_hi
        basis[:, 128:256] = p_lo
        g2 = jnp.dot(bh[...], basis[...], preferred_element_type=F32)
        g2 = g2[:, :128] + g2[:, 128:]
        g2 = g2 + jnp.dot(bl[...], basis[:, 0:128], preferred_element_type=F32)
        e = jnp.zeros((NR, 128), F32)
        for n in range(NKD):
            e = e + pltpu.roll(g2[n * NR : (n + 1) * NR, :], (n - KD - 16) % 128, 1)
        pos = lane((NR, 128))
        e_l = jnp.where(pos < 20, e, 0.0)
        e_r = jnp.where(pos >= 108, pltpu.roll(e, 76, 1), 0.0)
        return acc - jnp.concatenate([e_l, e_r], axis=1), pltpu.roll(v, WIN - PAD, 1)[:, :OWN]

    def base(n):
        arrived(wsem_r.at[n], lambda g: win.at[n, g])
        q, own = project(n)
        kept = own - q
        for g in range(8):
            cols[n, g] = kept[4 * g : 4 * g + 4, :]
        return spread(
            qsem_s.at[n], qsem_r.at[n], lambda g: cols.at[n, g], lambda g: own_columns(brow.at[n], g)
        )

    def base_rows(n):
        arrived(qsem_r.at[n], lambda g: own_columns(brow.at[n], g))
        return brow[n]

    at = sub((8, C))

    def eight(rows):
        return jnp.concatenate([rows[0:1], rows, jnp.zeros((3, C), F32)], axis=0)

    def smooth(n, half, sent):
        hbox[n] = half
        moves = [
            (hbox.at[n], hz.at[n, 0], {"wide": down_w}),
            (hbox.at[n], hz.at[n, 1], {"wide": up_w}),
            (hbox.at[n, 3], hrow.at[n, 2], {"wide": down_w, "grp": next_g}),
            (hbox.at[n, 0], hrow.at[n, 3], {"wide": up_w, "grp": last_g}),
            (hbox.at[n, 3], hrow.at[n, 0], {"grp": next_g}),
            (hbox.at[n, 0], hrow.at[n, 1], {"grp": last_g}),
        ]
        copies = []
        for m, (src, dst, who) in enumerate(moves):
            copy = pltpu.make_async_remote_copy(
                src_ref=src,
                dst_ref=dst,
                send_sem=hsem_s.at[n, m],
                recv_sem=hsem_r.at[n, m],
                device_id=who,
                device_id_type=MESH,
            )
            copy.start()
            copies.append(copy)
        for copy in sent:
            copy.wait_send()
        for copy in copies:
            copy.wait_recv()
        rows = hrow[n]
        mid = jnp.where(at == 0, rows[0:1], jnp.where(at == 5, rows[1:2], eight(half)))
        up = jnp.where(at == 0, rows[2:3], eight(hz[n, 0]))
        down = jnp.where(at == 5, rows[3:4], eight(hz[n, 1]))
        return (mid + TV_STEP * tv_rows(mid, up, down, wide, 4 * grp))[1:5], copies

    sent_q = base(0)

    pltpu.make_async_copy(buf, buf, asem_r).wait()
    for q in range(2):
        cut = slice(q * 1024, (q + 1) * 1024)
        to = slice(128 + q * 1024, 128 + (q + 1) * 1024)
        hi, lo = halves(buf[:, cut])
        xb[0:64, to], xb[64:128, to], xb[128:192, to], xb[192:256, to] = hi, lo, hi, lo

    def multiply(rel):
        w = wts[rel * NK * 16 : (rel + 1) * NK * 16, :]
        for t in range(WIDE // 256):
            big[:, t * 256 : (t + 1) * 256] = jnp.dot(
                w, xb[:, t * 256 : (t + 1) * 256], preferred_element_type=F32
            )

    def partial_rows(half):
        acc = jnp.zeros((8, C), F32)
        for k in range(NK):
            g = big[k * 16 + half * 8 : k * 16 + half * 8 + 8, :]
            acc = acc + pltpu.roll(g, (k - KB) % WIDE, 1)[:, 128 : 128 + C]
        return acc

    multiply(0)
    pairs = []
    for half in range(2):
        psend[half] = partial_rows(half)
        pair = pltpu.make_async_remote_copy(
            src_ref=psend.at[half],
            dst_ref=precv.at[half],
            send_sem=psem_s.at[half],
            recv_sem=psem_r.at[half],
            device_id={"grp": grp ^ 1},
            device_id_type=MESH,
        )
        pair.start()
        pairs.append(pair)
    multiply(1)
    for half in range(2):
        tile = partial_rows(half)
        pairs[half].wait_recv()
        tile = tile + precv[half]
        rsend[2 * half] = tile[0:4]
        rsend[2 * half + 1] = tile[4:8]
        for q in (2 * half, 2 * half + 1):
            mine = (zh == zl) & (zl == q)

            @pl.when(mine)
            def _():
                pltpu.make_async_copy(rsend.at[q], rrecv.at[zh], rsem_r.at[zh]).start()

            @pl.when(jnp.logical_not(mine))
            def _():
                pltpu.make_async_remote_copy(
                    src_ref=rsend.at[q],
                    dst_ref=rrecv.at[zh],
                    send_sem=rsem_s.at[q],
                    recv_sem=rsem_r.at[zh],
                    device_id=device(x, zl, y, q, c),
                    device_id_type=MESH,
                ).start()

    half1 = base_rows(0)
    for q in range(4):
        pltpu.make_async_copy(rrecv.at[q], rrecv.at[q], rsem_r.at[q]).wait()
    b = (rrecv[0] + rrecv[1]) + (rrecv[2] + rrecv[3])
    v1, sent_h = smooth(0, half1 + b, sent_w)
    pad_columns(v1)

    sent_w = spread(wsem_s.at[1], wsem_r.at[1], window, lambda g: win.at[1, g])
    sent_q = sent_q + base(1)
    pltpu.make_async_copy(buf, buf, asem_s).wait()
    for q in range(4):

        @pl.when(jnp.logical_not((zh == zl) & (zl == q)))
        def _():
            pltpu.make_async_copy(rsend.at[q], rsend.at[q], rsem_s.at[q]).wait()

    v2, sent = smooth(1, base_rows(1) + b, pairs + sent_h + sent_w + sent_q)
    out[0] = v2
    for copy in sent:
        copy.wait_send()


def on_device(measured, drift, start_volume):
    scale, slots, t4, f_hi, f_lo, b_hi, b_lo = tables()
    vmem = pl.BlockSpec(memory_space=pltpu.VMEM)
    hbm = pl.BlockSpec(memory_space=pltpu.HBM)
    dma = pltpu.SemaphoreType.DMA
    scratch = [
        pltpu.VMEM(t4.shape, BF16),
        pltpu.VMEM(f_hi.shape, BF16),
        pltpu.VMEM(f_lo.shape, BF16),
        pltpu.VMEM(b_hi.shape, BF16),
        pltpu.VMEM(b_lo.shape, BF16),
        pltpu.VMEM((64, C), F32),
        pltpu.VMEM((8, C), F32),
        pltpu.VMEM((2 * NK * 16, 256), BF16),
        pltpu.VMEM((256, WIDE), BF16),
        pltpu.VMEM((NK * 16, WIDE), F32),
        pltpu.VMEM((2, 8, C), F32),
        pltpu.VMEM((2, 8, C), F32),
        pltpu.VMEM((4, 4, C), F32),
        pltpu.VMEM((4, 4, C), F32),
        pltpu.VMEM((4, C + 128), F32),
        pltpu.VMEM((2, 8, 4, WIN), F32),
        pltpu.VMEM((128, WIN), BF16),
        pltpu.VMEM((NJ * NR, WIN), F32),
        pltpu.VMEM((NKP * NR, 256), BF16),
        pltpu.VMEM((A, 128), F32),
        pltpu.VMEM((A, 256), BF16),
        pltpu.VMEM((2, 8, 4, OWN), F32),
        pltpu.VMEM((2, 4, C), F32),
        pltpu.VMEM((2, 4, C), F32),
        pltpu.VMEM((2, 2, 4, C), F32),
        pltpu.VMEM((2, 4, C), F32),
        dma((5,)),
        dma,
        dma,
        dma((2,)),
        dma((2,)),
        dma((4,)),
        dma((4,)),
        dma((2, 8)),
        dma((2, 8)),
        dma((2, 8)),
        dma((2, 8)),
        dma((2, 6)),
        dma((2, 6)),
    ]
    return pl.pallas_call(
        functools.partial(kernel, float(scale)),
        out_shape=jax.ShapeDtypeStruct(start_volume.shape, F32),
        in_specs=[hbm, vmem, vmem, vmem] + [hbm] * 5,
        out_specs=vmem,
        scratch_shapes=scratch,
        compiler_params=pltpu.CompilerParams(
            collective_id=0, has_side_effects=True, vmem_limit_bytes=2**26 - 2**18
        ),
        name="sirt",
    )(
        measured,
        drift.reshape(4, 128),
        start_volume,
        jnp.asarray(slots),
        *(jnp.asarray(t) for t in (t4, f_hi, f_lo, b_hi, b_lo)),
    )


def solution(mesh):
    in_specs = (P(("wide", "grp"), None, None), P(), P("wide", "grp", None))
    return jax.shard_map(
        on_device, mesh=mesh, in_specs=in_specs, out_specs=P("wide", "grp", None), check_vma=False
    )
```

```python
import functools
import math

import jax
import jax.numpy as jnp
import ml_dtypes
import numpy as np
from jax import lax
from jax.experimental import pallas as pl
from jax.experimental.pallas import tpu as pltpu
from jax.sharding import PartitionSpec as P

MESH = pl.DeviceIdType.MESH
A = 512
C = 2048
Z = 64
NR = 32
DMAX = 4
EPS = 0.05
TV_STEP = 0.1
KB = 20
NK = 2 * KB + 1
KD = 16
NKD = 2 * KD + 1
NKP = 36
JT = 32
NJ = 2 * JT + 1
PAD = 64
WIN = 384
OWN = 256
WIDE = 128 + C + 128
HALF = C // 2
SPAN = 128 + HALF + 128
CUTS = ((0, HALF + 128), (HALF + 128, HALF - 128))
F32 = jnp.float32
BF16 = jnp.bfloat16


def tables():
    angle = (math.pi / 4) * (2.0 * np.arange(A) / (A - 1) - 1.0)
    tan, sec = np.tan(angle), 1.0 / np.cos(angle)
    scale = 1.0 / sec.sum() / NR
    height = np.arange(NR) - (NR - 1) / 2.0
    offsets = np.arange(-KD, KD + 1)
    tri = np.maximum(0.0, 1.0 - np.abs(height[None, :, None] * tan[:, None, None] - offsets))
    t = np.zeros((NJ, NR, NR))
    for n, j in enumerate(range(-JT, JT + 1)):
        lo, hi = max(-KD, -KD - j), min(KD, KD - j)
        if lo <= hi:
            k = np.arange(lo, hi + 1) + KD
            left = np.transpose(tri[:, :, k] * sec[:, None, None], (1, 0, 2)).reshape(NR, -1)
            right = np.transpose(tri[:, :, k + j], (1, 0, 2)).reshape(NR, -1)
            t[n] = left @ right.T
    t *= scale

    def split(x):
        x = x.astype(np.float32)
        hi = x.astype(ml_dtypes.bfloat16)
        return hi, (x - hi.astype(np.float32)).astype(ml_dtypes.bfloat16)

    t_hi, t_lo = split(t.reshape(NJ * NR, NR))
    t4 = np.concatenate([t_hi, t_hi, t_lo, t_lo], axis=1)
    kr = np.transpose(tri, (0, 2, 1)).reshape(A, NKD * NR)
    front = np.zeros((A, NKP * NR))
    front[:, : NKD * NR] = kr * sec[:, None]
    f_hi, f_lo = split(front)
    b_hi, b_lo = split(kr.T * scale)
    slots = np.zeros((8, 64))
    for zh in range(4):
        for c in range(2):
            for s in range(64):
                x, zl, y = s // 16, (s // 4) % 4, s % 4
                slots[zh * 2 + c, s] = tan[(x * 16 + zh * 4 + y) * 8 + zl * 2 + c]
    slots = np.tile(slots, (1, 4)).astype(np.float32)
    return scale, slots, t4, f_hi, f_lo, b_hi, b_lo


def halves(x):
    hi = x.astype(BF16)
    return hi, (x - hi.astype(F32)).astype(BF16)


def place():
    wide, grp = lax.axis_index("wide"), lax.axis_index("grp")
    return wide // 16, (wide // 4) % 4, wide % 4, grp // 2, grp % 2


def device(x, zh, y, zl, c):
    return {"wide": x * 16 + zh * 4 + y, "grp": zl * 2 + c}


def summed(zh, zl):
    far = 1 - zl // 2
    return (zh + 2 * far + 1 - ((zl % 2) ^ (1 - far))) % 4


def summer(zh, to):
    d = (to - zh + 4) % 4
    high = 1 - d // 2
    return 2 * high + 1 - ((d % 2) ^ high)


def lane(shape):
    return lax.broadcasted_iota(jnp.int32, shape, len(shape) - 1)


def sub(shape):
    return lax.broadcasted_iota(jnp.int32, shape, 0)


def tv_rows(mid, up, down, z, row0):
    shape = mid.shape
    row = row0 - 1 + sub(shape)
    inside = (row >= 0) & (row < NR - 1)
    last = lane(shape) < C - 1

    def units(centre, above):
        dr = jnp.where(inside, pltpu.roll(centre, 7, 0) - centre, 0.0)
        dc = jnp.where(last, pltpu.roll(centre, C - 1, 1) - centre, 0.0)
        inv = lax.rsqrt(above * above + dr * dr + dc * dc + EPS * EPS)
        return dr, dc, inv

    dz = jnp.where(z < Z - 1, up - mid, 0.0)
    dr, dc, inv = units(mid, dz)
    uz, ur, uc = dz * inv, dr * inv, dc * inv
    dz_b = jnp.where(z > 0, mid - down, 0.0)
    _, _, inv_b = units(down, dz_b)
    uc_b = jnp.where(lane(shape) > 0, pltpu.roll(uc, 1, 1), 0.0)
    return uz - dz_b * inv_b + (ur - pltpu.roll(ur, 1, 0)) + (uc - uc_b)


def kernel(
    scale,
    meas, drift, v0, slots, t4_h, fh_h, fl_h, bh_h, bl_h,
    out,
    t4, fh, fl, bh, bl, buf, spare, wts, xb, big,
    psend, precv, rsend, rrecv,
    vpad, win, rhs, gt, im, dcol, basis, cols, brow,
    hbox, hz, hrow,
    csem, asem_s, asem_r, psem_s, psem_r, rsem_s, rsem_r, wsem_s, wsem_r, qsem_s, qsem_r, hsem_s, hsem_r,
):
    wide, grp = lax.axis_index("wide"), lax.axis_index("grp")
    x, zh, y, zl, c = place()
    up_w, down_w = (wide + 1) % Z, (wide + Z - 1) % Z
    next_g, last_g = (grp + 1) % 8, (grp + 7) % 8

    def block_peer(i):
        px, pl_, py = x ^ ((i // 4) % 4), zl ^ (3 - i // 16), y ^ (i % 4)
        return device(px, zh, py, pl_, c), px * 16 + summed(zh, pl_) * 4 + py

    barrier = pltpu.get_barrier_semaphore()

    def hello(who):
        pl.semaphore_signal(barrier, inc=1, device_id=who, device_id_type=MESH)

    def greet(i, carry):
        hello(block_peer(i)[0])
        return carry

    goal = summed(zh, zl)
    away = zh != goal
    for who in (
        {"wide": up_w},
        {"wide": down_w},
        {"wide": down_w, "grp": next_g},
        {"wide": up_w, "grp": last_g},
    ):
        hello(who)
    for i in range(1, 4):
        hello(device(x, zh ^ i, y, summer(zh ^ i, zh), c))

    @pl.when(away)
    def _():
        for q in range(4):
            hello(device(x, goal, y, q, c))

    lax.fori_loop(0, 48, greet, 0)
    lax.fori_loop(49, 64, greet, 0)
    for q in range(4):
        hello(device(x, zh, y, q, 1 - c))

    loads = [
        pltpu.make_async_copy(src, dst, csem.at[n])
        for n, (src, dst) in enumerate(
            ((fh_h, fh), (fl_h, fl), (bh_h, bh), (bl_h, bl), (t4_h, t4))
        )
    ]
    for load in loads:
        load.start()

    def pad_columns(rows):
        vpad[...] = pltpu.roll(
            jnp.concatenate([rows, jnp.zeros((4, 128), F32)], axis=1), PAD, 1
        )

    pad_columns(v0[0])
    pl.semaphore_wait(barrier, 63 + 4 + 3 + 4 + jnp.where(away, 4, 0))

    me_slot, me_row = x * 16 + zl * 4 + y, x * 16 + goal * 4 + y

    def give(part):
        cut = pl.ds(*CUTS[part])

        def one(i, carry):
            who, row = block_peer(i)
            pltpu.make_async_remote_copy(
                src_ref=meas.at[0, row, cut],
                dst_ref=buf.at[me_slot, cut],
                send_sem=asem_s.at[part],
                recv_sem=asem_r.at[part],
                device_id=who,
                device_id_type=MESH,
            ).start()
            return carry

        lax.fori_loop(0, 48, one, 0)
        lax.fori_loop(49, 64, one, 0)
        mine = meas.at[0, me_row, cut]
        pltpu.make_async_copy(mine, buf.at[me_slot, cut], asem_r.at[part]).start()
        pltpu.make_async_copy(mine, spare.at[part, cut], asem_s.at[part]).start()

    def given(part, sem):
        cut = buf.at[:, pl.ds(*CUTS[part])]
        pltpu.make_async_copy(cut, cut, sem.at[part]).wait()

    def spread(sem_s, sem_r, source, target):
        pltpu.make_async_copy(source(grp), target(grp), sem_r.at[grp]).start()
        copies = []
        for i in range(7, 0, -1):
            peer = grp ^ i
            copy = pltpu.make_async_remote_copy(
                src_ref=source(peer),
                dst_ref=target(grp),
                send_sem=sem_s.at[i],
                recv_sem=sem_r.at[grp],
                device_id={"grp": peer},
                device_id_type=MESH,
            )
            copy.start()
            copies.append(copy)
        return copies

    def arrived(sem_r, target):
        for g in range(8):
            pltpu.make_async_copy(target(g), target(g), sem_r.at[g]).wait()

    def window(g):
        return vpad.at[:, pl.ds(pl.multiple_of(g * OWN, OWN), WIN)]

    def own_columns(ref, g):
        return ref.at[:, pl.ds(pl.multiple_of(g * OWN, OWN), OWN)]

    sent_w = spread(wsem_s.at[0], wsem_r.at[0], window, lambda g: win.at[0, g])
    give(0)
    give(1)

    for q in range(4):
        eye = sub((128, 128)) == lane((128, 128))
        line = jnp.broadcast_to(drift[q : q + 1, :].astype(F32), (128, 128))
        dcol[q * 128 : (q + 1) * 128, :] = jnp.broadcast_to(
            jnp.sum(jnp.where(eye, line, 0.0), axis=1, keepdims=True), (128, 128)
        )
    s = lane((8, 128)) % 64
    view = ((s // 16) * 16 + zh * 4 + s % 4) * 8 + ((s // 4) % 4) * 2 + c

    total = jnp.zeros((8, 128), F32)
    view_b = jnp.broadcast_to(view[0:1, :], (128, 128))
    for q in range(4):
        hit = view_b == (q * 128 + sub((128, 128)))
        total = total + jnp.sum(
            jnp.where(hit, dcol[q * 128 : (q + 1) * 128, :], 0.0), axis=0, keepdims=True
        )
    shift_d = jnp.concatenate([total[0:1], total[0:1]], axis=1)
    tan = slots[pl.ds(zh * 2 + c, 1), :]

    def weigh(n, carry):
        rel, k = n // NK, n % NK
        core = jnp.where(rel == 0, 1 - c, c)
        t = sub((16, 256))
        r = (t // 4) * 8 + core * 4 + t % 4
        height = r.astype(F32) - (NR - 1) / 2.0
        w = (
            jnp.maximum(0.0, 1.0 - jnp.abs(height * tan - shift_d - (k - KB).astype(F32))) * scale
        )
        hi = w.astype(BF16)
        lo = (w - hi.astype(F32)).astype(BF16)
        wts[pl.ds(pl.multiple_of(n * 16, 16), 16), :] = jnp.where(
            lane((16, 256)) < 128, hi.astype(F32), lo.astype(F32)
        ).astype(BF16)
        return carry

    lax.fori_loop(0, 2 * NK, weigh, 0)
    xb[:, 0:128] = jnp.zeros((256, 128), BF16)
    xb[:, WIDE - 128 :] = jnp.zeros((256, 128), BF16)
    im[...] = jnp.zeros_like(im)

    for load in loads:
        load.wait()

    def project(slot):
        v = jnp.concatenate([win[slot, g] for g in range(8)], axis=0)
        hi, lo = halves(v)
        rhs[0:32], rhs[32:64], rhs[64:96], rhs[96:128] = hi, lo, hi, lo
        gt[...] = jnp.dot(t4[...], rhs[...], preferred_element_type=F32)
        acc = jnp.zeros((NR, OWN), F32)
        for n in range(NJ):
            g = gt[n * NR : (n + 1) * NR, :]
            acc = acc + pltpu.roll(g, WIN - (PAD + n - JT), 1)[:, :OWN]
        for n in range(NKD):
            k = n - KD
            left = pltpu.roll(v, WIN - (48 + k), 1)[:, :128]
            right = pltpu.roll(v, WIN - (252 + k), 1)[:, :128]
            e = jnp.where(lane((NR, 128)) < 64, left, right)
            e_hi, e_lo = halves(e)
            im[n * NR : (n + 1) * NR, 0:128] = e_hi
            im[n * NR : (n + 1) * NR, 128:256] = e_lo
        p2 = jnp.dot(fh[...], im[...], preferred_element_type=F32)
        p = p2[:, :128] + p2[:, 128:] + jnp.dot(fl[...], im[:, 0:128], preferred_element_type=F32)
        pos = lane((A, 128))
        d = dcol[...]
        at = pos.astype(F32)
        cut_l = (grp == 0) & (pos < 20) & (at - 16.0 < -d)
        cut_r = (grp == 7) & (pos >= 64) & (pos < 84) & (at - 64.0 > 3.0 - d)
        p = jnp.where(cut_l | cut_r, p, 0.0)
        p_hi, p_lo = halves(p)
        basis[:, 0:128] = p_hi
        basis[:, 128:256] = p_lo
        g2 = jnp.dot(bh[...], basis[...], preferred_element_type=F32)
        g2 = g2[:, :128] + g2[:, 128:]
        g2 = g2 + jnp.dot(bl[...], basis[:, 0:128], preferred_element_type=F32)
        e = jnp.zeros((NR, 128), F32)
        for n in range(NKD):
            e = e + pltpu.roll(g2[n * NR : (n + 1) * NR, :], (n - KD - 16) % 128, 1)
        pos = lane((NR, 128))
        e_l = jnp.where(pos < 20, e, 0.0)
        e_r = jnp.where(pos >= 108, pltpu.roll(e, 76, 1), 0.0)
        return acc - jnp.concatenate([e_l, e_r], axis=1), pltpu.roll(v, WIN - PAD, 1)[:, :OWN]

    def base(n):
        arrived(wsem_r.at[n], lambda g: win.at[n, g])
        q, own = project(n)
        kept = own - q
        for g in range(8):
            cols[n, g] = kept[4 * g : 4 * g + 4, :]
        return spread(
            qsem_s.at[n], qsem_r.at[n], lambda g: cols.at[n, g], lambda g: own_columns(brow.at[n], g)
        )

    def base_rows(n, part):
        for g in range(4 * part, 4 * part + 4):
            piece = own_columns(brow.at[n], g)
            pltpu.make_async_copy(piece, piece, qsem_r.at[n, g]).wait()
        return brow[n, :, part * HALF : (part + 1) * HALF]

    at = sub((8, C))

    def eight(rows):
        return jnp.concatenate([rows[0:1], rows, jnp.zeros((3, C), F32)], axis=0)

    def share(n, part, half):
        cut = pl.ds(part * HALF, HALF)
        hbox[n, :, part * HALF : (part + 1) * HALF] = half
        moves = [
            (hbox.at[n, :, cut], hz.at[n, 0, :, cut], {"wide": down_w}),
            (hbox.at[n, :, cut], hz.at[n, 1, :, cut], {"wide": up_w}),
            (hbox.at[n, 3, cut], hrow.at[n, 2, cut], {"wide": down_w, "grp": next_g}),
            (hbox.at[n, 0, cut], hrow.at[n, 3, cut], {"wide": up_w, "grp": last_g}),
            (hbox.at[n, 3, cut], hrow.at[n, 0, cut], {"grp": next_g}),
            (hbox.at[n, 0, cut], hrow.at[n, 1, cut], {"grp": last_g}),
        ]
        copies = []
        for m, (src, dst, who) in enumerate(moves):
            copy = pltpu.make_async_remote_copy(
                src_ref=src,
                dst_ref=dst,
                send_sem=hsem_s.at[n, part, m],
                recv_sem=hsem_r.at[n, part, m],
                device_id=who,
                device_id_type=MESH,
            )
            copy.start()
            copies.append(copy)
        return copies

    def smooth(n, copies, sent):
        for copy in sent:
            copy.wait_send()
        for copy in copies:
            copy.wait_recv()
        rows = hrow[n]
        mid = jnp.where(at == 0, rows[0:1], jnp.where(at == 5, rows[1:2], eight(hbox[n])))
        up = jnp.where(at == 0, rows[2:3], eight(hz[n, 0]))
        down = jnp.where(at == 5, rows[3:4], eight(hz[n, 1]))
        return (mid + TV_STEP * tv_rows(mid, up, down, wide, 4 * grp))[1:5]

    sent_q = base(0)

    pairs = []

    def load_bins(part):
        given(part, asem_r)
        first, size = CUTS[part]
        to = slice(128 + first, 128 + first + size)
        hi, lo = halves(buf[:, first : first + size])
        xb[0:64, to], xb[64:128, to], xb[128:192, to], xb[192:256, to] = hi, lo, hi, lo

    def multiply(rel, part):
        w = wts[rel * NK * 16 : (rel + 1) * NK * 16, :]
        for t in range(SPAN // 256):
            first = part * HALF + t * 256
            big[:, t * 256 : (t + 1) * 256] = jnp.dot(
                w, xb[:, first : first + 256], preferred_element_type=F32
            )

    def partial_rows(half):
        acc = jnp.zeros((8, HALF), F32)
        for k in range(NK):
            g = big[k * 16 + half * 8 : k * 16 + half * 8 + 8, :]
            acc = acc + pltpu.roll(g, (k - KB) % SPAN, 1)[:, 128 : 128 + HALF]
        return acc

    for part in range(2):
        load_bins(part)
        multiply(0, part)
        for half in range(2):
            psend[part, half] = partial_rows(half)
            pair = pltpu.make_async_remote_copy(
                src_ref=psend.at[part, half],
                dst_ref=precv.at[part, half],
                send_sem=psem_s.at[part, half],
                recv_sem=psem_r.at[part, half],
                device_id={"grp": grp ^ 1},
                device_id_type=MESH,
            )
            pair.start()
            pairs.append(pair)
        multiply(1, part)
        for half in range(2):
            tile = partial_rows(half)
            pairs[2 * part + half].wait_recv()
            tile = tile + precv[part, half]
            rsend[part, 2 * half] = tile[0:4]
            rsend[part, 2 * half + 1] = tile[4:8]
            for q in (2 * half, 2 * half + 1):
                mine = (zh == goal) & (zl == q)

                @pl.when(mine)
                def _():
                    pltpu.make_async_copy(
                        rsend.at[part, q], rrecv.at[part, zh], rsem_r.at[part, zh]
                    ).start()

                @pl.when(jnp.logical_not(mine))
                def _():
                    pltpu.make_async_remote_copy(
                        src_ref=rsend.at[part, q],
                        dst_ref=rrecv.at[part, zh],
                        send_sem=rsem_s.at[part, q],
                        recv_sem=rsem_r.at[part, zh],
                        device_id=device(x, goal, y, q, c),
                        device_id_type=MESH,
                    ).start()

    b, shared = [], []
    for part in range(2):
        half1 = base_rows(0, part)
        for q in range(4):
            piece = rrecv.at[part, q]
            pltpu.make_async_copy(piece, piece, rsem_r.at[part, q]).wait()
        b.append((rrecv[part, 0] + rrecv[part, 1]) + (rrecv[part, 2] + rrecv[part, 3]))
        shared += share(0, part, half1 + b[part])
    v1 = smooth(0, shared, sent_w)
    pad_columns(v1)

    sent_w = spread(wsem_s.at[1], wsem_r.at[1], window, lambda g: win.at[1, g])
    sent_q = sent_q + base(1)
    sent = pairs + shared + sent_w + sent_q
    shared = []
    for part in range(2):
        shared += share(1, part, base_rows(1, part) + b[part])
    for part in range(2):
        given(part, asem_s)
        for q in range(4):

            @pl.when(jnp.logical_not((zh == goal) & (zl == q)))
            def _():
                piece = rsend.at[part, q]
                pltpu.make_async_copy(piece, piece, rsem_s.at[part, q]).wait()

    out[0] = smooth(1, shared, sent)
    for copy in shared:
        copy.wait_send()


def on_device(measured, drift, start_volume):
    scale, slots, t4, f_hi, f_lo, b_hi, b_lo = tables()
    vmem = pl.BlockSpec(memory_space=pltpu.VMEM)
    hbm = pl.BlockSpec(memory_space=pltpu.HBM)
    dma = pltpu.SemaphoreType.DMA
    scratch = [
        pltpu.VMEM(t4.shape, BF16),
        pltpu.VMEM(f_hi.shape, BF16),
        pltpu.VMEM(f_lo.shape, BF16),
        pltpu.VMEM(b_hi.shape, BF16),
        pltpu.VMEM(b_lo.shape, BF16),
        pltpu.VMEM((64, C), F32),
        pltpu.VMEM((8, C), F32),
        pltpu.VMEM((2 * NK * 16, 256), BF16),
        pltpu.VMEM((256, WIDE), BF16),
        pltpu.VMEM((NK * 16, SPAN), F32),
        pltpu.VMEM((2, 2, 8, HALF), F32),
        pltpu.VMEM((2, 2, 8, HALF), F32),
        pltpu.VMEM((2, 4, 4, HALF), F32),
        pltpu.VMEM((2, 4, 4, HALF), F32),
        pltpu.VMEM((4, C + 128), F32),
        pltpu.VMEM((2, 8, 4, WIN), F32),
        pltpu.VMEM((128, WIN), BF16),
        pltpu.VMEM((NJ * NR, WIN), F32),
        pltpu.VMEM((NKP * NR, 256), BF16),
        pltpu.VMEM((A, 128), F32),
        pltpu.VMEM((A, 256), BF16),
        pltpu.VMEM((2, 8, 4, OWN), F32),
        pltpu.VMEM((2, 4, C), F32),
        pltpu.VMEM((2, 4, C), F32),
        pltpu.VMEM((2, 2, 4, C), F32),
        pltpu.VMEM((2, 4, C), F32),
        dma((5,)),
        dma((2,)),
        dma((2,)),
        dma((2, 2)),
        dma((2, 2)),
        dma((2, 4)),
        dma((2, 4)),
        dma((2, 8)),
        dma((2, 8)),
        dma((2, 8)),
        dma((2, 8)),
        dma((2, 2, 6)),
        dma((2, 2, 6)),
    ]
    return pl.pallas_call(
        functools.partial(kernel, float(scale)),
        out_shape=jax.ShapeDtypeStruct(start_volume.shape, F32),
        in_specs=[hbm, vmem, vmem, vmem] + [hbm] * 5,
        out_specs=vmem,
        scratch_shapes=scratch,
        compiler_params=pltpu.CompilerParams(
            collective_id=0, has_side_effects=True, vmem_limit_bytes=2**26 - 2**18
        ),
        name="sirt",
    )(
        measured,
        drift.reshape(4, 128),
        start_volume,
        jnp.asarray(slots),
        *(jnp.asarray(t) for t in (t4, f_hi, f_lo, b_hi, b_lo)),
    )


def solution(mesh):
    in_specs = (P(("wide", "grp"), None, None), P(), P("wide", "grp", None))
    return jax.shard_map(
        on_device, mesh=mesh, in_specs=in_specs, out_specs=P("wide", "grp", None), check_vma=False
    )
```

```python
import functools
import math

import jax
import jax.numpy as jnp
import ml_dtypes
import numpy as np
from jax import lax
from jax.experimental import pallas as pl
from jax.experimental.pallas import tpu as pltpu
from jax.sharding import PartitionSpec as P

MESH = pl.DeviceIdType.MESH
A = 512
C = 2048
Z = 64
NR = 32
DMAX = 4
EPS = 0.05
TV_STEP = 0.1
KB = 20
NK = 2 * KB + 1
KD = 16
NKD = 2 * KD + 1
NKP = 36
JT = 32
NJ = 2 * JT + 1
PAD = 128
HALO = 64
WIN = 384
WIN0 = 512
OWN = 256
WIDE = 128 + C + 128
HALF = C // 2
SPAN = 128 + HALF + 128
REACH = HALF + 128
CUTS = ((0, HALF + 128), (HALF + 128, HALF - 128))
F32 = jnp.float32
BF16 = jnp.bfloat16


def tables():
    angle = (math.pi / 4) * (2.0 * np.arange(A) / (A - 1) - 1.0)
    tan, sec = np.tan(angle), 1.0 / np.cos(angle)
    scale = 1.0 / sec.sum() / NR
    height = np.arange(NR) - (NR - 1) / 2.0
    offsets = np.arange(-KD, KD + 1)
    tri = np.maximum(0.0, 1.0 - np.abs(height[None, :, None] * tan[:, None, None] - offsets))
    t = np.zeros((NJ, NR, NR))
    for n, j in enumerate(range(-JT, JT + 1)):
        lo, hi = max(-KD, -KD - j), min(KD, KD - j)
        if lo <= hi:
            k = np.arange(lo, hi + 1) + KD
            left = np.transpose(tri[:, :, k] * sec[:, None, None], (1, 0, 2)).reshape(NR, -1)
            right = np.transpose(tri[:, :, k + j], (1, 0, 2)).reshape(NR, -1)
            t[n] = left @ right.T
    t *= scale

    def split(x):
        x = x.astype(np.float32)
        hi = x.astype(ml_dtypes.bfloat16)
        return hi, (x - hi.astype(np.float32)).astype(ml_dtypes.bfloat16)

    t_hi, t_lo = split(t.reshape(NJ * NR, NR))
    t4 = np.concatenate([t_hi, t_hi, t_lo, t_lo], axis=1)
    kr = np.transpose(tri, (0, 2, 1)).reshape(A, NKD * NR)
    front = np.zeros((A, NKP * NR))
    front[:, : NKD * NR] = kr * sec[:, None]
    f_hi, b_hi = split(front)[0], split(kr.T * scale)[0]
    slots = np.zeros((8, 64))
    for zh in range(4):
        for c in range(2):
            for s in range(64):
                x, zl, y = s // 16, (s // 4) % 4, s % 4
                slots[zh * 2 + c, s] = tan[(x * 16 + zh * 4 + y) * 8 + zl * 2 + c]
    slots = np.tile(slots, (1, 4)).astype(np.float32)
    return scale, slots, t4, f_hi, b_hi


def halves(x):
    hi = x.astype(BF16)
    return hi, (x - hi.astype(F32)).astype(BF16)


def place():
    wide, grp = lax.axis_index("wide"), lax.axis_index("grp")
    return wide // 16, (wide // 4) % 4, wide % 4, grp // 2, grp % 2


def device(x, zh, y, zl, c):
    return {"wide": x * 16 + zh * 4 + y, "grp": zl * 2 + c}


def summed(zh, zl):
    far = 1 - zl // 2
    return (zh + 2 * far + 1 - ((zl % 2) ^ (1 - far))) % 4


def summer(zh, to):
    d = (to - zh + 4) % 4
    high = 1 - d // 2
    return 2 * high + 1 - ((d % 2) ^ high)


def lane(shape):
    return lax.broadcasted_iota(jnp.int32, shape, len(shape) - 1)


def sub(shape):
    return lax.broadcasted_iota(jnp.int32, shape, 0)


def tv_rows(mid, up, down, z, row0):
    shape = mid.shape
    row = row0 - 1 + sub(shape)
    inside = (row >= 0) & (row < NR - 1)
    last = lane(shape) < C - 1

    def units(centre, above):
        dr = jnp.where(inside, pltpu.roll(centre, 7, 0) - centre, 0.0)
        dc = jnp.where(last, pltpu.roll(centre, C - 1, 1) - centre, 0.0)
        inv = lax.rsqrt(above * above + dr * dr + dc * dc + EPS * EPS)
        return dr, dc, inv

    dz = jnp.where(z < Z - 1, up - mid, 0.0)
    dr, dc, inv = units(mid, dz)
    uz, ur, uc = dz * inv, dr * inv, dc * inv
    dz_b = jnp.where(z > 0, mid - down, 0.0)
    _, _, inv_b = units(down, dz_b)
    uc_b = jnp.where(lane(shape) > 0, pltpu.roll(uc, 1, 1), 0.0)
    return uz - dz_b * inv_b + (ur - pltpu.roll(ur, 1, 0)) + (uc - uc_b)


def tv_window(mid, up, down, z, column0):
    shape = mid.shape
    column = column0 + lane(shape)
    below = sub(shape) < NR - 1
    inside = (column >= 0) & (column < C - 1)

    def units(centre, dz):
        dr = jnp.where(below, pltpu.roll(centre, NR - 1, 0) - centre, 0.0)
        dc = jnp.where(inside, pltpu.roll(centre, shape[1] - 1, 1) - centre, 0.0)
        return dr, dc, lax.rsqrt(dz * dz + dr * dr + dc * dc + EPS * EPS)

    dz = jnp.where(z < Z - 1, up - mid, 0.0)
    dr, dc, inv = units(mid, dz)
    uz, ur, uc = dz * inv, dr * inv, dc * inv
    dz_b = jnp.where(z > 0, mid - down, 0.0)
    _, _, inv_b = units(down, dz_b)
    return uz - dz_b * inv_b + (ur - pltpu.roll(ur, 1, 0)) + (uc - pltpu.roll(uc, 1, 1))


def begin(src, dst, send_sem, recv_sem, who):
    copy = pltpu.make_async_remote_copy(
        src_ref=src,
        dst_ref=dst,
        send_sem=send_sem,
        recv_sem=recv_sem,
        device_id=who,
        device_id_type=MESH,
    )
    copy.start()
    return copy


def kernel(
    scale,
    meas, drift, v0, slots, t4_h, fh_h, bh_h,
    out,
    t4, fh, bh, buf, spare, wts, xb, big,
    sums, precv, rsend, rrecv,
    vpad, win, rhs, gt, im, dcol, basis, cols,
    hwin, zwin, hbox, hz, hrow,
    csem, asem_s, asem_r, psem_s, psem_r, rsem_s, rsem_r, wsem_s, wsem_r, qsem_s, qsem_r, zsem_s, zsem_r, hsem_s, hsem_r,
):
    wide, grp = lax.axis_index("wide"), lax.axis_index("grp")
    x, zh, y, zl, c = place()
    up_w, down_w = (wide + 1) % Z, (wide + Z - 1) % Z
    next_g, last_g = (grp + 1) % 8, (grp + 7) % 8

    def block_peer(i):
        px, pl_, py = x ^ ((i // 4) % 4), zl ^ (3 - i // 16), y ^ (i % 4)
        return device(px, zh, py, pl_, c), px * 16 + summed(zh, pl_) * 4 + py

    barrier = pltpu.get_barrier_semaphore()

    def hello(who):
        pl.semaphore_signal(barrier, inc=1, device_id=who, device_id_type=MESH)

    def greet(i, carry):
        hello(block_peer(i)[0])
        return carry

    goal = summed(zh, zl)
    away = zh != goal
    for who in (
        {"wide": up_w},
        {"wide": down_w},
        {"wide": down_w, "grp": next_g},
        {"wide": up_w, "grp": last_g},
    ):
        hello(who)
    for i in range(1, 4):
        hello(device(x, zh ^ i, y, summer(zh ^ i, zh), c))

    @pl.when(away)
    def _():
        for q in range(4):
            hello(device(x, goal, y, q, c))

    lax.fori_loop(0, 48, greet, 0)
    lax.fori_loop(49, 64, greet, 0)
    for q in range(4):
        hello(device(x, zh, y, q, 1 - c))

    loads = [
        pltpu.make_async_copy(src, dst, csem.at[n])
        for n, (src, dst) in enumerate(((fh_h, fh), (bh_h, bh), (t4_h, t4)))
    ]
    for load in loads:
        load.start()

    vpad[:, :PAD] = jnp.zeros((4, PAD), F32)
    vpad[:, PAD : PAD + C] = v0[0]
    vpad[:, PAD + C :] = jnp.zeros((4, PAD), F32)
    pl.semaphore_wait(barrier, 63 + 4 + 3 + 4 + jnp.where(away, 4, 0))

    me_slot, me_row = x * 16 + zl * 4 + y, x * 16 + goal * 4 + y

    def give(part):
        cut = pl.ds(*CUTS[part])

        def one(i, carry):
            who, row = block_peer(i)
            pltpu.make_async_remote_copy(
                src_ref=meas.at[0, row, cut],
                dst_ref=buf.at[me_slot, cut],
                send_sem=asem_s.at[part],
                recv_sem=asem_r.at[part],
                device_id=who,
                device_id_type=MESH,
            ).start()
            return carry

        lax.fori_loop(0, 48, one, 0)
        lax.fori_loop(49, 64, one, 0)
        mine = meas.at[0, me_row, cut]
        pltpu.make_async_copy(mine, buf.at[me_slot, cut], asem_r.at[part]).start()
        pltpu.make_async_copy(mine, spare.at[part, cut], asem_s.at[part]).start()

    def given(part, sem):
        cut = buf.at[:, pl.ds(*CUTS[part])]
        pltpu.make_async_copy(cut, cut, sem.at[part]).wait()

    def spread(sem_s, sem_r, source, target):
        pltpu.make_async_copy(source(grp), target(grp), sem_r.at[grp]).start()
        copies = []
        for i in range(7, 0, -1):
            peer = grp ^ i
            copy = pltpu.make_async_remote_copy(
                src_ref=source(peer),
                dst_ref=target(grp),
                send_sem=sem_s.at[i],
                recv_sem=sem_r.at[grp],
                device_id={"grp": peer},
                device_id_type=MESH,
            )
            copy.start()
            copies.append(copy)
        return copies

    def arrived(sem_r, target):
        for g in range(8):
            pltpu.make_async_copy(target(g), target(g), sem_r.at[g]).wait()

    def window(g):
        return vpad.at[:, pl.ds(pl.multiple_of(g * OWN, OWN), WIN0)]

    def own_columns(ref, g):
        return ref.at[:, pl.ds(pl.multiple_of(g * OWN, OWN), OWN)]

    sent_w = spread(wsem_s, wsem_r, window, lambda g: win.at[g])
    give(0)
    give(1)

    for q in range(4):
        eye = sub((128, 128)) == lane((128, 128))
        line = jnp.broadcast_to(drift[q : q + 1, :].astype(F32), (128, 128))
        dcol[q * 128 : (q + 1) * 128, :] = jnp.broadcast_to(
            jnp.sum(jnp.where(eye, line, 0.0), axis=1, keepdims=True), (128, 128)
        )
    s = lane((8, 128)) % 64
    view = ((s // 16) * 16 + zh * 4 + s % 4) * 8 + ((s // 4) % 4) * 2 + c

    total = jnp.zeros((8, 128), F32)
    view_b = jnp.broadcast_to(view[0:1, :], (128, 128))
    for q in range(4):
        hit = view_b == (q * 128 + sub((128, 128)))
        total = total + jnp.sum(
            jnp.where(hit, dcol[q * 128 : (q + 1) * 128, :], 0.0), axis=0, keepdims=True
        )
    shift_d = jnp.concatenate([total[0:1], total[0:1]], axis=1)
    tan = slots[pl.ds(zh * 2 + c, 1), :]

    def weigh(n, carry):
        k, upper = n // 2, n % 2
        height = (upper * 16 + sub((16, 256))).astype(F32) - (NR - 1) / 2.0
        w = (
            jnp.maximum(0.0, 1.0 - jnp.abs(height * tan - shift_d - (k - KB).astype(F32))) * scale
        )
        hi = w.astype(BF16)
        lo = (w - hi.astype(F32)).astype(BF16)
        wts[pl.ds(pl.multiple_of(n * 16, 16), 16), :] = jnp.where(
            lane((16, 256)) < 128, hi.astype(F32), lo.astype(F32)
        ).astype(BF16)
        return carry

    lax.fori_loop(0, 2 * NK, weigh, 0)
    xb[:, 0:128] = jnp.zeros((256, 128), BF16)
    xb[:, WIDE - 128 :] = jnp.zeros((256, 128), BF16)
    im[...] = jnp.zeros_like(im)

    for load in loads:
        load.wait()

    def project(v):
        size = v.shape[1]
        kept = size - 2 * HALO
        hi, lo = halves(v)
        rhs[0:32, :size], rhs[32:64, :size] = hi, lo
        rhs[64:96, :size], rhs[96:128, :size] = hi, lo
        gt[:, :size] = jnp.dot(t4[...], rhs[:, :size], preferred_element_type=F32)
        acc = jnp.zeros((NR, kept), F32)
        for n in range(NJ):
            g = gt[n * NR : (n + 1) * NR, :size]
            acc = acc + pltpu.roll(g, size - (HALO + n - JT), 1)[:, :kept]
        zero, top = size // 2 - OWN // 2, size // 2 - OWN // 2 + 2044 - 7 * OWN
        head, tail = v[:, :256], v[:, size - 256 :]
        for n in range(NKD):
            k = n - KD
            left = pltpu.roll(head, (256 - (zero - 16 + k)) % 256, 1)[:, :128]
            right = pltpu.roll(tail, (256 - (top - (size - 256) - 64 + k)) % 256, 1)[:, :128]
            e = jnp.where(lane((NR, 128)) < 64, left, right)
            e_hi, e_lo = halves(e)
            im[n * NR : (n + 1) * NR, 0:128] = e_hi
            im[n * NR : (n + 1) * NR, 128:256] = e_lo
        p2 = jnp.dot(fh[...], im[...], preferred_element_type=F32)
        p = p2[:, :128] + p2[:, 128:]
        pos = lane((A, 128))
        d = dcol[...]
        at = pos.astype(F32)
        cut_l = (grp == 0) & (pos < 20) & (at - 16.0 < -d)
        cut_r = (grp == 7) & (pos >= 64) & (pos < 84) & (at - 64.0 > 3.0 - d)
        p = jnp.where(cut_l | cut_r, p, 0.0)
        p_hi, p_lo = halves(p)
        basis[:, 0:128] = p_hi
        basis[:, 128:256] = p_lo
        g2 = jnp.dot(bh[...], basis[...], preferred_element_type=F32)
        g2 = g2[:, :128] + g2[:, 128:]
        e = jnp.zeros((NR, 128), F32)
        for n in range(NKD):
            e = e + pltpu.roll(g2[n * NR : (n + 1) * NR, :], (n - KD - 16) % 128, 1)
        pos = lane((NR, 128))
        start, move = zero - HALO, top - HALO - 48 - (kept - 128)
        e_l = jnp.where((pos >= start) & (pos < start + 20), pltpu.roll(e, start, 1), 0.0)
        e_r = jnp.where((pos >= 32 + move) & (pos < 52 + move), pltpu.roll(e, move, 1), 0.0)
        edges = [e_l] + [jnp.zeros((NR, 128), F32)] * (kept // 128 - 2) + [e_r]
        return acc - jnp.concatenate(edges, axis=1)

    at = sub((8, C))

    def eight(rows):
        return jnp.concatenate([rows[0:1], rows, jnp.zeros((3, C), F32)], axis=0)

    def share(part):
        for g in range(4 * part, 4 * part + 4):
            piece = own_columns(hbox, g)
            pltpu.make_async_copy(piece, piece, qsem_r.at[g]).wait()
        cut = pl.ds(part * HALF, HALF)
        moves = [
            (hbox.at[:, cut], hz.at[0, :, cut], {"wide": down_w}),
            (hbox.at[:, cut], hz.at[1, :, cut], {"wide": up_w}),
            (hbox.at[3, cut], hrow.at[2, cut], {"wide": down_w, "grp": next_g}),
            (hbox.at[0, cut], hrow.at[3, cut], {"wide": up_w, "grp": last_g}),
            (hbox.at[3, cut], hrow.at[0, cut], {"grp": next_g}),
            (hbox.at[0, cut], hrow.at[1, cut], {"grp": last_g}),
        ]
        return [
            begin(src, dst, hsem_s.at[part, m], hsem_r.at[part, m], who)
            for m, (src, dst, who) in enumerate(moves)
        ]

    arrived(wsem_r, lambda g: win.at[g])
    v = jnp.concatenate([win[g] for g in range(8)], axis=0)
    hwin[...] = v[:, HALO : HALO + WIN] - project(v)

    pairs = []

    def load_bins(part):
        given(part, asem_r)
        first, size = CUTS[part]
        to = slice(128 + first, 128 + first + size)
        hi, lo = halves(buf[:, first : first + size])
        xb[0:64, to], xb[64:128, to], xb[128:192, to], xb[192:256, to] = hi, lo, hi, lo

    def of_part(n):
        return pl.ds(pl.multiple_of(n * OWN, OWN), WIN)

    for part in range(2):
        load_bins(part)
        for t in range(SPAN // 256):
            first = part * HALF + t * 256
            big[:, t * 256 : (t + 1) * 256] = jnp.dot(
                wts[...], xb[:, first : first + 256], preferred_element_type=F32
            )
        for tile in range(4):
            acc = jnp.zeros((8, REACH), F32)
            for k in range(NK):
                g = big[k * NR + tile * 8 : k * NR + tile * 8 + 8, :]
                acc = acc + pltpu.roll(g, (k - KB - HALO) % SPAN, 1)[:, :REACH]
            sums[part, tile * 8 : tile * 8 + 8, :] = acc
        for n in range(2):
            pairs.append(
                begin(
                    sums.at[part, :, of_part(2 * n + 1 - c)],
                    precv.at[part, n],
                    psem_s.at[part, n],
                    psem_r.at[part, n],
                    {"grp": grp ^ 1},
                )
            )
        for n in range(2):
            q = 2 * part + n
            pairs[q].wait_recv()
            rsend[q] = sums[part, :, of_part(2 * n + c)] + precv[part, n]
            mine = (zh == goal) & (zl == q)

            @pl.when(mine)
            def _():
                pltpu.make_async_copy(rsend.at[q], rrecv.at[zh], rsem_r.at[zh]).start()

            @pl.when(jnp.logical_not(mine))
            def _():
                begin(
                    rsend.at[q],
                    rrecv.at[zh],
                    rsem_s.at[q],
                    rsem_r.at[zh],
                    device(x, goal, y, q, c),
                )

    for q in range(4):
        pltpu.make_async_copy(rrecv.at[q], rrecv.at[q], rsem_r.at[q]).wait()
    b = (rrecv[0] + rrecv[1]) + (rrecv[2] + rrecv[3])
    half1 = hwin[...] + b
    hwin[...] = half1
    near = [
        begin(hwin, zwin.at[0], zsem_s.at[0], zsem_r.at[0], {"wide": down_w}),
        begin(hwin, zwin.at[1], zsem_s.at[1], zsem_r.at[1], {"wide": up_w}),
    ]
    for copy in near:
        copy.wait_recv()
    v1 = half1 + TV_STEP * tv_window(half1, zwin[0], zwin[1], wide, grp * OWN - HALO)
    column = grp * OWN - HALO + lane((NR, WIN))
    v1 = jnp.where((column >= 0) & (column < C), v1, 0.0)

    half2 = (v1 + b)[:, HALO : HALO + OWN] - project(v1)
    for g in range(8):
        cols[g] = half2[4 * g : 4 * g + 4, :]
    sent_q = spread(qsem_s, qsem_r, lambda g: cols.at[g], lambda g: own_columns(hbox, g))
    shared = share(0) + share(1)
    for copy in sent_w + pairs + near + sent_q:
        copy.wait_send()
    for part in range(2):
        given(part, asem_s)
    for q in range(4):

        @pl.when(jnp.logical_not((zh == goal) & (zl == q)))
        def _():
            pltpu.make_async_copy(rsend.at[q], rsend.at[q], rsem_s.at[q]).wait()

    for copy in shared:
        copy.wait_recv()
    rows = hrow[...]
    mid = jnp.where(at == 0, rows[0:1], jnp.where(at == 5, rows[1:2], eight(hbox[...])))
    up = jnp.where(at == 0, rows[2:3], eight(hz[0]))
    down = jnp.where(at == 5, rows[3:4], eight(hz[1]))
    out[0] = (mid + TV_STEP * tv_rows(mid, up, down, wide, 4 * grp))[1:5]
    for copy in shared:
        copy.wait_send()


def on_device(measured, drift, start_volume):
    scale, slots, t4, f_hi, b_hi = tables()
    vmem = pl.BlockSpec(memory_space=pltpu.VMEM)
    hbm = pl.BlockSpec(memory_space=pltpu.HBM)
    dma = pltpu.SemaphoreType.DMA
    scratch = [
        pltpu.VMEM(t4.shape, BF16),
        pltpu.VMEM(f_hi.shape, BF16),
        pltpu.VMEM(b_hi.shape, BF16),
        pltpu.VMEM((64, C), F32),
        pltpu.VMEM((8, C), F32),
        pltpu.VMEM((NK * NR, 256), BF16),
        pltpu.VMEM((256, WIDE), BF16),
        pltpu.VMEM((NK * NR, SPAN), F32),
        pltpu.VMEM((2, NR, REACH), F32),
        pltpu.VMEM((2, 2, NR, WIN), F32),
        pltpu.VMEM((4, NR, WIN), F32),
        pltpu.VMEM((4, NR, WIN), F32),
        pltpu.VMEM((4, C + 2 * PAD), F32),
        pltpu.VMEM((8, 4, WIN0), F32),
        pltpu.VMEM((128, WIN0), BF16),
        pltpu.VMEM((NJ * NR, WIN0), F32),
        pltpu.VMEM((NKP * NR, 256), BF16),
        pltpu.VMEM((A, 128), F32),
        pltpu.VMEM((A, 256), BF16),
        pltpu.VMEM((8, 4, OWN), F32),
        pltpu.VMEM((NR, WIN), F32),
        pltpu.VMEM((2, NR, WIN), F32),
        pltpu.VMEM((4, C), F32),
        pltpu.VMEM((2, 4, C), F32),
        pltpu.VMEM((4, C), F32),
        dma((3,)),
        dma((2,)),
        dma((2,)),
        dma((2, 2)),
        dma((2, 2)),
        dma((4,)),
        dma((4,)),
        dma((8,)),
        dma((8,)),
        dma((8,)),
        dma((8,)),
        dma((2,)),
        dma((2,)),
        dma((2, 6)),
        dma((2, 6)),
    ]
    return pl.pallas_call(
        functools.partial(kernel, float(scale)),
        out_shape=jax.ShapeDtypeStruct(start_volume.shape, F32),
        in_specs=[hbm, vmem, vmem, vmem] + [hbm] * 3,
        out_specs=vmem,
        scratch_shapes=scratch,
        compiler_params=pltpu.CompilerParams(
            collective_id=0, has_side_effects=True, vmem_limit_bytes=2**26 - 2**18
        ),
        name="sirt",
    )(
        measured,
        drift.reshape(4, 128),
        start_volume,
        jnp.asarray(slots),
        *(jnp.asarray(t) for t in (t4, f_hi, b_hi)),
    )


def solution(mesh):
    in_specs = (P(("wide", "grp"), None, None), P(), P("wide", "grp", None))
    return jax.shard_map(
        on_device, mesh=mesh, in_specs=in_specs, out_specs=P("wide", "grp", None), check_vma=False
    )
```

```python
import functools
import math

import jax
import jax.numpy as jnp
import ml_dtypes
import numpy as np
from jax import lax
from jax.experimental import pallas as pl
from jax.experimental.pallas import tpu as pltpu
from jax.sharding import PartitionSpec as P

MESH = pl.DeviceIdType.MESH
A = 512
C = 2048
Z = 64
NR = 32
DMAX = 4
EPS = 0.05
TV_STEP = 0.1
KB = 20
NK = 2 * KB + 1
KD = 16
NKD = 2 * KD + 1
NKP = 36
JT = 32
NJ = 2 * JT + 1
PAD = 64
WIN = 384
OWN = 256
WIDE = 128 + C + 128
HALF = C // 2
SPAN = 128 + HALF + 128
CUTS = ((0, HALF + 128), (HALF + 128, HALF - 128))
F32 = jnp.float32
BF16 = jnp.bfloat16


def tables():
    angle = (math.pi / 4) * (2.0 * np.arange(A) / (A - 1) - 1.0)
    tan, sec = np.tan(angle), 1.0 / np.cos(angle)
    scale = 1.0 / sec.sum() / NR
    height = np.arange(NR) - (NR - 1) / 2.0
    offsets = np.arange(-KD, KD + 1)
    tri = np.maximum(0.0, 1.0 - np.abs(height[None, :, None] * tan[:, None, None] - offsets))
    t = np.zeros((NJ, NR, NR))
    for n, j in enumerate(range(-JT, JT + 1)):
        lo, hi = max(-KD, -KD - j), min(KD, KD - j)
        if lo <= hi:
            k = np.arange(lo, hi + 1) + KD
            left = np.transpose(tri[:, :, k] * sec[:, None, None], (1, 0, 2)).reshape(NR, -1)
            right = np.transpose(tri[:, :, k + j], (1, 0, 2)).reshape(NR, -1)
            t[n] = left @ right.T
    t *= scale

    def split(x):
        x = x.astype(np.float32)
        hi = x.astype(ml_dtypes.bfloat16)
        return hi, (x - hi.astype(np.float32)).astype(ml_dtypes.bfloat16)

    t_hi, t_lo = split(t.reshape(NJ * NR, NR))
    t4 = np.concatenate([t_hi, t_hi, t_lo, t_lo], axis=1)
    kr = np.transpose(tri, (0, 2, 1)).reshape(A, NKD * NR)
    front = np.zeros((A, NKP * NR))
    front[:, : NKD * NR] = kr * sec[:, None]
    f_hi, b_hi = split(front)[0], split(kr.T * scale)[0]
    slots = np.zeros((8, 64))
    for zh in range(4):
        for c in range(2):
            for s in range(64):
                x, zl, y = s // 16, (s // 4) % 4, s % 4
                slots[zh * 2 + c, s] = tan[(x * 16 + zh * 4 + y) * 8 + zl * 2 + c]
    slots = np.tile(slots, (1, 4)).astype(np.float32)
    return scale, slots, t4, f_hi, b_hi


def halves(x):
    hi = x.astype(BF16)
    return hi, (x - hi.astype(F32)).astype(BF16)


def place():
    wide, grp = lax.axis_index("wide"), lax.axis_index("grp")
    return wide // 16, (wide // 4) % 4, wide % 4, grp // 2, grp % 2


def device(x, zh, y, zl, c):
    return {"wide": x * 16 + zh * 4 + y, "grp": zl * 2 + c}


def summed(zh, zl):
    far = 1 - zl // 2
    return (zh + 2 * far + 1 - ((zl % 2) ^ (1 - far))) % 4


def summer(zh, to):
    d = (to - zh + 4) % 4
    high = 1 - d // 2
    return 2 * high + 1 - ((d % 2) ^ high)


def lane(shape):
    return lax.broadcasted_iota(jnp.int32, shape, len(shape) - 1)


def sub(shape):
    return lax.broadcasted_iota(jnp.int32, shape, 0)


def tv_rows(mid, up, down, z, row0):
    shape = mid.shape
    row = row0 - 1 + sub(shape)
    inside = (row >= 0) & (row < NR - 1)
    last = lane(shape) < C - 1

    def units(centre, above):
        dr = jnp.where(inside, pltpu.roll(centre, 7, 0) - centre, 0.0)
        dc = jnp.where(last, pltpu.roll(centre, C - 1, 1) - centre, 0.0)
        inv = lax.rsqrt(above * above + dr * dr + dc * dc + EPS * EPS)
        return dr, dc, inv

    dz = jnp.where(z < Z - 1, up - mid, 0.0)
    dr, dc, inv = units(mid, dz)
    uz, ur, uc = dz * inv, dr * inv, dc * inv
    dz_b = jnp.where(z > 0, mid - down, 0.0)
    _, _, inv_b = units(down, dz_b)
    uc_b = jnp.where(lane(shape) > 0, pltpu.roll(uc, 1, 1), 0.0)
    return uz - dz_b * inv_b + (ur - pltpu.roll(ur, 1, 0)) + (uc - uc_b)


def kernel(
    scale,
    meas, drift, v0, slots, t4_h, fh_h, bh_h,
    out,
    t4, fh, bh, buf, spare, wts, xb, big,
    psend, precv, rsend, rrecv,
    vpad, win, rhs, gt, im, dcol, basis, cols, brow,
    hbox, hz, hrow,
    csem, asem_s, asem_r, psem_s, psem_r, rsem_s, rsem_r, wsem_s, wsem_r, qsem_s, qsem_r, hsem_s, hsem_r,
):
    wide, grp = lax.axis_index("wide"), lax.axis_index("grp")
    x, zh, y, zl, c = place()
    up_w, down_w = (wide + 1) % Z, (wide + Z - 1) % Z
    next_g, last_g = (grp + 1) % 8, (grp + 7) % 8

    def block_peer(i):
        px, pl_, py = x ^ ((i // 4) % 4), zl ^ (3 - i // 16), y ^ (i % 4)
        return device(px, zh, py, pl_, c), px * 16 + summed(zh, pl_) * 4 + py

    barrier = pltpu.get_barrier_semaphore()

    def hello(who):
        pl.semaphore_signal(barrier, inc=1, device_id=who, device_id_type=MESH)

    def greet(i, carry):
        hello(block_peer(i)[0])
        return carry

    goal = summed(zh, zl)
    away = zh != goal
    for who in (
        {"wide": up_w},
        {"wide": down_w},
        {"wide": down_w, "grp": next_g},
        {"wide": up_w, "grp": last_g},
    ):
        hello(who)
    for i in range(1, 4):
        hello(device(x, zh ^ i, y, summer(zh ^ i, zh), c))

    @pl.when(away)
    def _():
        for q in range(4):
            hello(device(x, goal, y, q, c))

    lax.fori_loop(0, 48, greet, 0, unroll=True)
    lax.fori_loop(49, 64, greet, 0, unroll=True)
    for q in range(4):
        hello(device(x, zh, y, q, 1 - c))

    loads = [
        pltpu.make_async_copy(src, dst, csem.at[n])
        for n, (src, dst) in enumerate(((fh_h, fh), (bh_h, bh), (t4_h, t4)))
    ]
    for load in loads:
        load.start()

    def pad_columns(rows):
        vpad[...] = pltpu.roll(
            jnp.concatenate([rows, jnp.zeros((4, 128), F32)], axis=1), PAD, 1
        )

    pad_columns(v0[0])
    pl.semaphore_wait(barrier, 63 + 4 + 3 + 4 + jnp.where(away, 4, 0))

    me_slot, me_row = x * 16 + zl * 4 + y, x * 16 + goal * 4 + y

    def give(part):
        cut = pl.ds(*CUTS[part])

        def one(i, carry):
            who, row = block_peer(i)
            pltpu.make_async_remote_copy(
                src_ref=meas.at[0, row, cut],
                dst_ref=buf.at[me_slot, cut],
                send_sem=asem_s.at[part],
                recv_sem=asem_r.at[part],
                device_id=who,
                device_id_type=MESH,
            ).start()
            return carry

        lax.fori_loop(0, 48, one, 0, unroll=True)
        lax.fori_loop(49, 64, one, 0, unroll=True)
        mine = meas.at[0, me_row, cut]
        pltpu.make_async_copy(mine, buf.at[me_slot, cut], asem_r.at[part]).start()
        pltpu.make_async_copy(mine, spare.at[part, cut], asem_s.at[part]).start()

    def given(part, sem):
        cut = buf.at[:, pl.ds(*CUTS[part])]
        pltpu.make_async_copy(cut, cut, sem.at[part]).wait()

    def spread(sem_s, sem_r, source, target):
        pltpu.make_async_copy(source(grp), target(grp), sem_r.at[grp]).start()
        copies = []
        for i in range(7, 0, -1):
            peer = grp ^ i
            copy = pltpu.make_async_remote_copy(
                src_ref=source(peer),
                dst_ref=target(grp),
                send_sem=sem_s.at[i],
                recv_sem=sem_r.at[grp],
                device_id={"grp": peer},
                device_id_type=MESH,
            )
            copy.start()
            copies.append(copy)
        return copies

    def arrived(sem_r, target):
        for g in range(8):
            pltpu.make_async_copy(target(g), target(g), sem_r.at[g]).wait()

    def window(g):
        return vpad.at[:, pl.ds(pl.multiple_of(g * OWN, OWN), WIN)]

    def own_columns(ref, g):
        return ref.at[:, pl.ds(pl.multiple_of(g * OWN, OWN), OWN)]

    sent_w = spread(wsem_s.at[0], wsem_r.at[0], window, lambda g: win.at[0, g])
    give(0)
    give(1)

    for q in range(4):
        eye = sub((128, 128)) == lane((128, 128))
        line = jnp.broadcast_to(drift[q : q + 1, :].astype(F32), (128, 128))
        dcol[q * 128 : (q + 1) * 128, :] = jnp.broadcast_to(
            jnp.sum(jnp.where(eye, line, 0.0), axis=1, keepdims=True), (128, 128)
        )
    s = lane((8, 128)) % 64
    view = ((s // 16) * 16 + zh * 4 + s % 4) * 8 + ((s // 4) % 4) * 2 + c

    total = jnp.zeros((8, 128), F32)
    view_b = jnp.broadcast_to(view[0:1, :], (128, 128))
    for q in range(4):
        hit = view_b == (q * 128 + sub((128, 128)))
        total = total + jnp.sum(
            jnp.where(hit, dcol[q * 128 : (q + 1) * 128, :], 0.0), axis=0, keepdims=True
        )
    shift_d = jnp.concatenate([total[0:1], total[0:1]], axis=1)
    tan = slots[pl.ds(zh * 2 + c, 1), :]

    def weigh(n, carry):
        rel, k = n // NK, n % NK
        core = jnp.where(rel == 0, 1 - c, c)
        t = sub((16, 256))
        r = (t // 4) * 8 + core * 4 + t % 4
        height = r.astype(F32) - (NR - 1) / 2.0
        w = (
            jnp.maximum(0.0, 1.0 - jnp.abs(height * tan - shift_d - (k - KB).astype(F32))) * scale
        )
        hi = w.astype(BF16)
        lo = (w - hi.astype(F32)).astype(BF16)
        wts[pl.ds(pl.multiple_of(n * 16, 16), 16), :] = jnp.where(
            lane((16, 256)) < 128, hi.astype(F32), lo.astype(F32)
        ).astype(BF16)
        return carry

    lax.fori_loop(0, 2 * NK, weigh, 0)
    xb[:, 0:128] = jnp.zeros((256, 128), BF16)
    xb[:, WIDE - 128 :] = jnp.zeros((256, 128), BF16)
    im[...] = jnp.zeros_like(im)

    for load in loads:
        load.wait()

    def project(slot):
        v = jnp.concatenate([win[slot, g] for g in range(8)], axis=0)
        hi, lo = halves(v)
        rhs[0:32], rhs[32:64], rhs[64:96], rhs[96:128] = hi, lo, hi, lo
        gt[...] = jnp.dot(t4[...], rhs[...], preferred_element_type=F32)
        acc = jnp.zeros((NR, OWN), F32)
        for n in range(NJ):
            g = gt[n * NR : (n + 1) * NR, :]
            acc = acc + pltpu.roll(g, WIN - (PAD + n - JT), 1)[:, :OWN]
        head, tail = v[:, :128], v[:, 256:]
        for n in range(NKD):
            k = n - KD
            left = pltpu.roll(head, 128 - (48 + k), 1)
            right = pltpu.roll(tail, (4 - k) % 128, 1)
            e = jnp.where(lane((NR, 128)) < 64, left, right)
            e_hi, e_lo = halves(e)
            im[n * NR : (n + 1) * NR, 0:128] = e_hi
            im[n * NR : (n + 1) * NR, 128:256] = e_lo
        p2 = jnp.dot(fh[...], im[...], preferred_element_type=F32)
        p = p2[:, :128] + p2[:, 128:]
        pos = lane((A, 128))
        d = dcol[...]
        at = pos.astype(F32)
        cut_l = (grp == 0) & (pos < 20) & (at - 16.0 < -d)
        cut_r = (grp == 7) & (pos >= 64) & (pos < 84) & (at - 64.0 > 3.0 - d)
        p = jnp.where(cut_l | cut_r, p, 0.0)
        p_hi, p_lo = halves(p)
        basis[:, 0:128] = p_hi
        basis[:, 128:256] = p_lo
        g2 = jnp.dot(bh[...], basis[...], preferred_element_type=F32)
        g2 = g2[:, :128] + g2[:, 128:]
        e = jnp.zeros((NR, 128), F32)
        for n in range(NKD):
            e = e + pltpu.roll(g2[n * NR : (n + 1) * NR, :], (n - KD - 16) % 128, 1)
        pos = lane((NR, 128))
        e_l = jnp.where(pos < 20, e, 0.0)
        e_r = jnp.where(pos >= 108, pltpu.roll(e, 76, 1), 0.0)
        return acc - jnp.concatenate([e_l, e_r], axis=1), pltpu.roll(v, WIN - PAD, 1)[:, :OWN]

    def base(n):
        arrived(wsem_r.at[n], lambda g: win.at[n, g])
        q, own = project(n)
        kept = own - q
        for g in range(8):
            cols[n, g] = kept[4 * g : 4 * g + 4, :]
        return spread(
            qsem_s.at[n], qsem_r.at[n], lambda g: cols.at[n, g], lambda g: own_columns(brow.at[n], g)
        )

    def base_rows(n, part):
        for g in range(4 * part, 4 * part + 4):
            piece = own_columns(brow.at[n], g)
            pltpu.make_async_copy(piece, piece, qsem_r.at[n, g]).wait()
        return brow[n, :, part * HALF : (part + 1) * HALF]

    at = sub((8, C))

    def eight(rows):
        return jnp.concatenate([rows[0:1], rows, jnp.zeros((3, C), F32)], axis=0)

    def share(n, part, half):
        cut = pl.ds(part * HALF, HALF)
        hbox[n, :, part * HALF : (part + 1) * HALF] = half
        moves = [
            (hbox.at[n, :, cut], hz.at[n, 0, :, cut], {"wide": down_w}),
            (hbox.at[n, :, cut], hz.at[n, 1, :, cut], {"wide": up_w}),
            (hbox.at[n, 3, cut], hrow.at[n, 2, cut], {"wide": down_w, "grp": next_g}),
            (hbox.at[n, 0, cut], hrow.at[n, 3, cut], {"wide": up_w, "grp": last_g}),
            (hbox.at[n, 3, cut], hrow.at[n, 0, cut], {"grp": next_g}),
            (hbox.at[n, 0, cut], hrow.at[n, 1, cut], {"grp": last_g}),
        ]
        copies = []
        for m, (src, dst, who) in enumerate(moves):
            copy = pltpu.make_async_remote_copy(
                src_ref=src,
                dst_ref=dst,
                send_sem=hsem_s.at[n, part, m],
                recv_sem=hsem_r.at[n, part, m],
                device_id=who,
                device_id_type=MESH,
            )
            copy.start()
            copies.append(copy)
        return copies

    def smooth(n, copies, sent):
        for copy in sent:
            copy.wait_send()
        for copy in copies:
            copy.wait_recv()
        rows = hrow[n]
        mid = jnp.where(at == 0, rows[0:1], jnp.where(at == 5, rows[1:2], eight(hbox[n])))
        up = jnp.where(at == 0, rows[2:3], eight(hz[n, 0]))
        down = jnp.where(at == 5, rows[3:4], eight(hz[n, 1]))
        return (mid + TV_STEP * tv_rows(mid, up, down, wide, 4 * grp))[1:5]

    sent_q = base(0)

    pairs = []

    def load_bins(part):
        given(part, asem_r)
        first, size = CUTS[part]
        to = slice(128 + first, 128 + first + size)
        hi, lo = halves(buf[:, first : first + size])
        xb[0:64, to], xb[64:128, to], xb[128:192, to], xb[192:256, to] = hi, lo, hi, lo

    def multiply(rel, part):
        w = wts[rel * NK * 16 : (rel + 1) * NK * 16, :]
        for t in range(SPAN // 256):
            first = part * HALF + t * 256
            big[:, t * 256 : (t + 1) * 256] = jnp.dot(
                w, xb[:, first : first + 256], preferred_element_type=F32
            )

    def partial_rows(half):
        acc = jnp.zeros((8, HALF), F32)
        for k in range(NK):
            g = big[k * 16 + half * 8 : k * 16 + half * 8 + 8, :]
            acc = acc + pltpu.roll(g, (k - KB) % SPAN, 1)[:, 128 : 128 + HALF]
        return acc

    for part in range(2):
        load_bins(part)
        multiply(0, part)
        for half in range(2):
            psend[part, half] = partial_rows(half)
            pair = pltpu.make_async_remote_copy(
                src_ref=psend.at[part, half],
                dst_ref=precv.at[part, half],
                send_sem=psem_s.at[part, half],
                recv_sem=psem_r.at[part, half],
                device_id={"grp": grp ^ 1},
                device_id_type=MESH,
            )
            pair.start()
            pairs.append(pair)
        multiply(1, part)
        for half in range(2):
            tile = partial_rows(half)
            pairs[2 * part + half].wait_recv()
            tile = tile + precv[part, half]
            rsend[part, 2 * half] = tile[0:4]
            rsend[part, 2 * half + 1] = tile[4:8]
            for q in (2 * half, 2 * half + 1):
                mine = (zh == goal) & (zl == q)

                @pl.when(mine)
                def _():
                    pltpu.make_async_copy(
                        rsend.at[part, q], rrecv.at[part, zh], rsem_r.at[part, zh]
                    ).start()

                @pl.when(jnp.logical_not(mine))
                def _():
                    pltpu.make_async_remote_copy(
                        src_ref=rsend.at[part, q],
                        dst_ref=rrecv.at[part, zh],
                        send_sem=rsem_s.at[part, q],
                        recv_sem=rsem_r.at[part, zh],
                        device_id=device(x, goal, y, q, c),
                        device_id_type=MESH,
                    ).start()

    b, shared = [], []
    for part in range(2):
        half1 = base_rows(0, part)
        for q in range(4):
            piece = rrecv.at[part, q]
            pltpu.make_async_copy(piece, piece, rsem_r.at[part, q]).wait()
        b.append((rrecv[part, 0] + rrecv[part, 1]) + (rrecv[part, 2] + rrecv[part, 3]))
        shared += share(0, part, half1 + b[part])
    v1 = smooth(0, shared, sent_w)
    pad_columns(v1)

    sent_w = spread(wsem_s.at[1], wsem_r.at[1], window, lambda g: win.at[1, g])
    sent_q = sent_q + base(1)
    sent = pairs + shared + sent_w + sent_q
    shared = []
    for part in range(2):
        shared += share(1, part, base_rows(1, part) + b[part])
    for part in range(2):
        given(part, asem_s)
        for q in range(4):

            @pl.when(jnp.logical_not((zh == goal) & (zl == q)))
            def _():
                piece = rsend.at[part, q]
                pltpu.make_async_copy(piece, piece, rsem_s.at[part, q]).wait()

    out[0] = smooth(1, shared, sent)
    for copy in shared:
        copy.wait_send()


def on_device(measured, drift, start_volume):
    scale, slots, t4, f_hi, b_hi = tables()
    vmem = pl.BlockSpec(memory_space=pltpu.VMEM)
    hbm = pl.BlockSpec(memory_space=pltpu.HBM)
    dma = pltpu.SemaphoreType.DMA
    scratch = [
        pltpu.VMEM(t4.shape, BF16),
        pltpu.VMEM(f_hi.shape, BF16),
        pltpu.VMEM(b_hi.shape, BF16),
        pltpu.VMEM((64, C), F32),
        pltpu.VMEM((8, C), F32),
        pltpu.VMEM((2 * NK * 16, 256), BF16),
        pltpu.VMEM((256, WIDE), BF16),
        pltpu.VMEM((NK * 16, SPAN), F32),
        pltpu.VMEM((2, 2, 8, HALF), F32),
        pltpu.VMEM((2, 2, 8, HALF), F32),
        pltpu.VMEM((2, 4, 4, HALF), F32),
        pltpu.VMEM((2, 4, 4, HALF), F32),
        pltpu.VMEM((4, C + 128), F32),
        pltpu.VMEM((2, 8, 4, WIN), F32),
        pltpu.VMEM((128, WIN), BF16),
        pltpu.VMEM((NJ * NR, WIN), F32),
        pltpu.VMEM((NKP * NR, 256), BF16),
        pltpu.VMEM((A, 128), F32),
        pltpu.VMEM((A, 256), BF16),
        pltpu.VMEM((2, 8, 4, OWN), F32),
        pltpu.VMEM((2, 4, C), F32),
        pltpu.VMEM((2, 4, C), F32),
        pltpu.VMEM((2, 2, 4, C), F32),
        pltpu.VMEM((2, 4, C), F32),
        dma((3,)),
        dma((2,)),
        dma((2,)),
        dma((2, 2)),
        dma((2, 2)),
        dma((2, 4)),
        dma((2, 4)),
        dma((2, 8)),
        dma((2, 8)),
        dma((2, 8)),
        dma((2, 8)),
        dma((2, 2, 6)),
        dma((2, 2, 6)),
    ]
    return pl.pallas_call(
        functools.partial(kernel, float(scale)),
        out_shape=jax.ShapeDtypeStruct(start_volume.shape, F32),
        in_specs=[hbm, vmem, vmem, vmem] + [hbm] * 3,
        out_specs=vmem,
        scratch_shapes=scratch,
        compiler_params=pltpu.CompilerParams(
            collective_id=0, has_side_effects=True, vmem_limit_bytes=2**26 - 2**18
        ),
        name="sirt",
    )(
        measured,
        drift.reshape(4, 128),
        start_volume,
        jnp.asarray(slots),
        *(jnp.asarray(t) for t in (t4, f_hi, b_hi)),
    )


def solution(mesh):
    in_specs = (P(("wide", "grp"), None, None), P(), P("wide", "grp", None))
    return jax.shard_map(
        on_device, mesh=mesh, in_specs=in_specs, out_specs=P("wide", "grp", None), check_vma=False
    )
```

```python
import functools
import math

import jax
import jax.numpy as jnp
import ml_dtypes
import numpy as np
from jax import lax
from jax.experimental import pallas as pl
from jax.experimental.pallas import tpu as pltpu
from jax.sharding import PartitionSpec as P

MESH = pl.DeviceIdType.MESH
A = 512
C = 2048
Z = 64
NR = 32
DMAX = 4
EPS = 0.05
TV_STEP = 0.1
KB = 20
NK = 2 * KB + 1
KD = 16
NKD = 2 * KD + 1
NKP = 36
JT = 32
NJ = 2 * JT + 1
PAD = 64
WIN = 384
OWN = 256
WIDE = 128 + C + 128
HALF = C // 2
SPAN = 128 + HALF + 128
CUTS = ((0, HALF + 128), (HALF + 128, HALF - 128))
F32 = jnp.float32
BF16 = jnp.bfloat16


def tables():
    angle = (math.pi / 4) * (2.0 * np.arange(A) / (A - 1) - 1.0)
    tan, sec = np.tan(angle), 1.0 / np.cos(angle)
    scale = 1.0 / sec.sum() / NR
    height = np.arange(NR) - (NR - 1) / 2.0
    offsets = np.arange(-KD, KD + 1)
    tri = np.maximum(0.0, 1.0 - np.abs(height[None, :, None] * tan[:, None, None] - offsets))
    t = np.zeros((NJ, NR, NR))
    for n, j in enumerate(range(-JT, JT + 1)):
        lo, hi = max(-KD, -KD - j), min(KD, KD - j)
        if lo <= hi:
            k = np.arange(lo, hi + 1) + KD
            left = np.transpose(tri[:, :, k] * sec[:, None, None], (1, 0, 2)).reshape(NR, -1)
            right = np.transpose(tri[:, :, k + j], (1, 0, 2)).reshape(NR, -1)
            t[n] = left @ right.T
    t *= scale

    def split(x):
        x = x.astype(np.float32)
        hi = x.astype(ml_dtypes.bfloat16)
        return hi, (x - hi.astype(np.float32)).astype(ml_dtypes.bfloat16)

    t_hi, t_lo = split(t.reshape(NJ * NR, NR))
    t4 = np.concatenate([t_hi, t_hi, t_lo, t_lo], axis=1)
    kr = np.transpose(tri, (0, 2, 1)).reshape(A, NKD * NR)
    front = np.zeros((A, NKP * NR))
    front[:, : NKD * NR] = kr * sec[:, None]
    f_hi, b_hi = split(front)[0], split(kr.T * scale)[0]
    slots = np.zeros((8, 64))
    for zh in range(4):
        for c in range(2):
            for s in range(64):
                x, zl, y = s // 16, (s // 4) % 4, s % 4
                slots[zh * 2 + c, s] = tan[(x * 16 + zh * 4 + y) * 8 + zl * 2 + c]
    slots = np.tile(slots, (1, 4)).astype(np.float32)
    return scale, slots, t4, f_hi, b_hi


def halves(x):
    hi = x.astype(BF16)
    return hi, (x - hi.astype(F32)).astype(BF16)


def place():
    wide, grp = lax.axis_index("wide"), lax.axis_index("grp")
    return wide // 16, (wide // 4) % 4, wide % 4, grp // 2, grp % 2


def device(x, zh, y, zl, c):
    return {"wide": x * 16 + zh * 4 + y, "grp": zl * 2 + c}


def summed(zh, zl):
    far = 1 - zl // 2
    return (zh + 2 * far + 1 - ((zl % 2) ^ (1 - far))) % 4


def summer(zh, to):
    d = (to - zh + 4) % 4
    high = 1 - d // 2
    return 2 * high + 1 - ((d % 2) ^ high)


def lane(shape):
    return lax.broadcasted_iota(jnp.int32, shape, len(shape) - 1)


def sub(shape):
    return lax.broadcasted_iota(jnp.int32, shape, 0)


def tv_rows(mid, up, down, z, row0):
    shape = mid.shape
    row = row0 - 1 + sub(shape)
    inside = (row >= 0) & (row < NR - 1)
    last = lane(shape) < C - 1

    def units(centre, above):
        dr = jnp.where(inside, pltpu.roll(centre, 7, 0) - centre, 0.0)
        dc = jnp.where(last, pltpu.roll(centre, C - 1, 1) - centre, 0.0)
        inv = lax.rsqrt(above * above + dr * dr + dc * dc + EPS * EPS)
        return dr, dc, inv

    dz = jnp.where(z < Z - 1, up - mid, 0.0)
    dr, dc, inv = units(mid, dz)
    uz, ur, uc = dz * inv, dr * inv, dc * inv
    dz_b = jnp.where(z > 0, mid - down, 0.0)
    _, _, inv_b = units(down, dz_b)
    uc_b = jnp.where(lane(shape) > 0, pltpu.roll(uc, 1, 1), 0.0)
    return uz - dz_b * inv_b + (ur - pltpu.roll(ur, 1, 0)) + (uc - uc_b)


def kernel(
    scale,
    meas, drift, v0, slots, t4_h, fh_h, bh_h,
    out,
    t4, fh, bh, buf, spare, wts, xb, big,
    psend, precv, rsend, rrecv,
    vpad, win, rhs, gt, im, dcol, basis, cols, brow,
    hbox, hz, hrow,
    csem, asem_s, asem_r, psem_s, psem_r, rsem_s, rsem_r, wsem_s, wsem_r, qsem_s, qsem_r, hsem_s, hsem_r,
):
    wide, grp = lax.axis_index("wide"), lax.axis_index("grp")
    x, zh, y, zl, c = place()
    up_w, down_w = (wide + 1) % Z, (wide + Z - 1) % Z
    next_g, last_g = (grp + 1) % 8, (grp + 7) % 8

    def block_peer(i):
        px, pl_, py = x ^ ((i // 4) % 4), zl ^ (3 - i // 16), y ^ (i % 4)
        return device(px, zh, py, pl_, c), px * 16 + summed(zh, pl_) * 4 + py

    barrier = pltpu.get_barrier_semaphore()

    def hello(who):
        pl.semaphore_signal(barrier, inc=1, device_id=who, device_id_type=MESH)

    def greet(i, carry):
        hello(block_peer(i)[0])
        return carry

    goal = summed(zh, zl)
    away = zh != goal
    for who in (
        {"wide": up_w},
        {"wide": down_w},
        {"wide": down_w, "grp": next_g},
        {"wide": up_w, "grp": last_g},
    ):
        hello(who)
    for i in range(1, 4):
        hello(device(x, zh ^ i, y, summer(zh ^ i, zh), c))

    @pl.when(away)
    def _():
        for q in range(4):
            hello(device(x, goal, y, q, c))

    lax.fori_loop(0, 48, greet, 0, unroll=True)
    lax.fori_loop(49, 64, greet, 0, unroll=True)
    for q in range(4):
        hello(device(x, zh, y, q, 1 - c))

    loads = [
        pltpu.make_async_copy(src, dst, csem.at[n])
        for n, (src, dst) in enumerate(((fh_h, fh), (bh_h, bh), (t4_h, t4)))
    ]
    for load in loads:
        load.start()

    def pad_columns(rows):
        vpad[...] = pltpu.roll(
            jnp.concatenate([rows, jnp.zeros((4, 128), F32)], axis=1), PAD, 1
        )

    pad_columns(v0[0])
    pl.semaphore_wait(barrier, 63 + 4 + 3 + 4 + jnp.where(away, 4, 0))

    me_slot, me_row = x * 16 + zl * 4 + y, x * 16 + goal * 4 + y

    def give(part):
        cut = pl.ds(*CUTS[part])

        def one(i, carry):
            who, row = block_peer(i)
            pltpu.make_async_remote_copy(
                src_ref=meas.at[0, row, cut],
                dst_ref=buf.at[me_slot, cut],
                send_sem=asem_s.at[part],
                recv_sem=asem_r.at[part],
                device_id=who,
                device_id_type=MESH,
            ).start()
            return carry

        lax.fori_loop(0, 48, one, 0, unroll=True)
        lax.fori_loop(49, 64, one, 0, unroll=True)
        mine = meas.at[0, me_row, cut]
        pltpu.make_async_copy(mine, buf.at[me_slot, cut], asem_r.at[part]).start()
        pltpu.make_async_copy(mine, spare.at[part, cut], asem_s.at[part]).start()

    def given(part, sem):
        cut = buf.at[:, pl.ds(*CUTS[part])]
        pltpu.make_async_copy(cut, cut, sem.at[part]).wait()

    def spread(sem_s, sem_r, source, target):
        pltpu.make_async_copy(source(grp), target(grp), sem_r.at[grp]).start()
        copies = []
        for i in range(7, 0, -1):
            peer = grp ^ i
            copy = pltpu.make_async_remote_copy(
                src_ref=source(peer),
                dst_ref=target(grp),
                send_sem=sem_s.at[i],
                recv_sem=sem_r.at[grp],
                device_id={"grp": peer},
                device_id_type=MESH,
            )
            copy.start()
            copies.append(copy)
        return copies

    def arrived(sem_r, target):
        for g in range(8):
            pltpu.make_async_copy(target(g), target(g), sem_r.at[g]).wait()

    def window(g):
        return vpad.at[:, pl.ds(pl.multiple_of(g * OWN, OWN), WIN)]

    def own_columns(ref, g):
        return ref.at[:, pl.ds(pl.multiple_of(g * OWN, OWN), OWN)]

    sent_w = spread(wsem_s.at[0], wsem_r.at[0], window, lambda g: win.at[0, g])
    give(0)
    give(1)

    for q in range(4):
        eye = sub((128, 128)) == lane((128, 128))
        line = jnp.broadcast_to(drift[q : q + 1, :].astype(F32), (128, 128))
        dcol[q * 128 : (q + 1) * 128, :] = jnp.broadcast_to(
            jnp.sum(jnp.where(eye, line, 0.0), axis=1, keepdims=True), (128, 128)
        )
    s = lane((8, 128)) % 64
    view = ((s // 16) * 16 + zh * 4 + s % 4) * 8 + ((s // 4) % 4) * 2 + c

    total = jnp.zeros((8, 128), F32)
    view_b = jnp.broadcast_to(view[0:1, :], (128, 128))
    for q in range(4):
        hit = view_b == (q * 128 + sub((128, 128)))
        total = total + jnp.sum(
            jnp.where(hit, dcol[q * 128 : (q + 1) * 128, :], 0.0), axis=0, keepdims=True
        )
    shift_d = jnp.concatenate([total[0:1], total[0:1]], axis=1)
    tan = slots[pl.ds(zh * 2 + c, 1), :]

    def weigh(n, carry):
        rel, k = n // NK, n % NK
        core = jnp.where(rel == 0, 1 - c, c)
        t = sub((16, 256))
        r = (t // 4) * 8 + core * 4 + t % 4
        height = r.astype(F32) - (NR - 1) / 2.0
        w = (
            jnp.maximum(0.0, 1.0 - jnp.abs(height * tan - shift_d - (k - KB).astype(F32))) * scale
        )
        hi = w.astype(BF16)
        lo = (w - hi.astype(F32)).astype(BF16)
        wts[pl.ds(pl.multiple_of(n * 16, 16), 16), :] = jnp.where(
            lane((16, 256)) < 128, hi.astype(F32), lo.astype(F32)
        ).astype(BF16)
        return carry

    lax.fori_loop(0, 2 * NK, weigh, 0)
    xb[:, 0:128] = jnp.zeros((256, 128), BF16)
    xb[:, WIDE - 128 :] = jnp.zeros((256, 128), BF16)
    im[...] = jnp.zeros_like(im)

    for load in loads:
        load.wait()

    def project(slot):
        v = jnp.concatenate([win[slot, g] for g in range(8)], axis=0)
        hi, lo = halves(v)
        rhs[0:32], rhs[32:64], rhs[64:96], rhs[96:128] = hi, lo, hi, lo
        gt[...] = jnp.dot(t4[...], rhs[...], preferred_element_type=F32)
        acc = jnp.zeros((NR, OWN), F32)
        for n in range(NJ):
            g = gt[n * NR : (n + 1) * NR, :]
            acc = acc + pltpu.roll(g, WIN - (PAD + n - JT), 1)[:, :OWN]
        head, tail = v[:, :128], v[:, 256:]
        for n in range(NKD):
            k = n - KD
            left = pltpu.roll(head, 128 - (48 + k), 1)
            right = pltpu.roll(tail, (4 - k) % 128, 1)
            e = jnp.where(lane((NR, 128)) < 64, left, right)
            e_hi, e_lo = halves(e)
            im[n * NR : (n + 1) * NR, 0:128] = e_hi
            im[n * NR : (n + 1) * NR, 128:256] = e_lo
        p2 = jnp.dot(fh[...], im[...], preferred_element_type=F32)
        p = p2[:, :128] + p2[:, 128:]
        pos = lane((A, 128))
        d = dcol[...]
        at = pos.astype(F32)
        cut_l = (grp == 0) & (pos < 20) & (at - 16.0 < -d)
        cut_r = (grp == 7) & (pos >= 64) & (pos < 84) & (at - 64.0 > 3.0 - d)
        p = jnp.where(cut_l | cut_r, p, 0.0)
        p_hi, p_lo = halves(p)
        basis[:, 0:128] = p_hi
        basis[:, 128:256] = p_lo
        g2 = jnp.dot(bh[...], basis[...], preferred_element_type=F32)
        g2 = g2[:, :128] + g2[:, 128:]
        e = jnp.zeros((NR, 128), F32)
        for n in range(NKD):
            e = e + pltpu.roll(g2[n * NR : (n + 1) * NR, :], (n - KD - 16) % 128, 1)
        pos = lane((NR, 128))
        e_l = jnp.where(pos < 20, e, 0.0)
        e_r = jnp.where(pos >= 108, pltpu.roll(e, 76, 1), 0.0)
        return acc - jnp.concatenate([e_l, e_r], axis=1), pltpu.roll(v, WIN - PAD, 1)[:, :OWN]

    def base(n):
        arrived(wsem_r.at[n], lambda g: win.at[n, g])
        q, own = project(n)
        kept = own - q
        for g in range(8):
            cols[n, g] = kept[4 * g : 4 * g + 4, :]
        return spread(
            qsem_s.at[n], qsem_r.at[n], lambda g: cols.at[n, g], lambda g: own_columns(brow.at[n], g)
        )

    def base_rows(n, part):
        for g in range(4 * part, 4 * part + 4):
            piece = own_columns(brow.at[n], g)
            pltpu.make_async_copy(piece, piece, qsem_r.at[n, g]).wait()
        return brow[n, :, part * HALF : (part + 1) * HALF]

    at = sub((8, C))

    def eight(rows):
        return jnp.concatenate([rows[0:1], rows, jnp.zeros((3, C), F32)], axis=0)

    def share(n, part, first, half):
        size = half.shape[1]
        cut = pl.ds(first, size)
        hbox[n, :, first : first + size] = half
        moves = [
            (hbox.at[n, :, cut], hz.at[n, 0, :, cut], {"wide": down_w}),
            (hbox.at[n, :, cut], hz.at[n, 1, :, cut], {"wide": up_w}),
            (hbox.at[n, 3, cut], hrow.at[n, 2, cut], {"wide": down_w, "grp": next_g}),
            (hbox.at[n, 0, cut], hrow.at[n, 3, cut], {"wide": up_w, "grp": last_g}),
            (hbox.at[n, 3, cut], hrow.at[n, 0, cut], {"grp": next_g}),
            (hbox.at[n, 0, cut], hrow.at[n, 1, cut], {"grp": last_g}),
        ]
        copies = []
        for m, (src, dst, who) in enumerate(moves):
            copy = pltpu.make_async_remote_copy(
                src_ref=src,
                dst_ref=dst,
                send_sem=hsem_s.at[n, part, m],
                recv_sem=hsem_r.at[n, part, m],
                device_id=who,
                device_id_type=MESH,
            )
            copy.start()
            copies.append(copy)
        return copies

    def smooth(n, copies, sent):
        for copy in sent:
            copy.wait_send()
        for copy in copies:
            copy.wait_recv()
        rows = hrow[n]
        mid = jnp.where(at == 0, rows[0:1], jnp.where(at == 5, rows[1:2], eight(hbox[n])))
        up = jnp.where(at == 0, rows[2:3], eight(hz[n, 0]))
        down = jnp.where(at == 5, rows[3:4], eight(hz[n, 1]))
        return (mid + TV_STEP * tv_rows(mid, up, down, wide, 4 * grp))[1:5]

    sent_q = base(0)

    pairs = []

    def load_bins(part):
        given(part, asem_r)
        first, size = CUTS[part]
        to = slice(128 + first, 128 + first + size)
        hi, lo = halves(buf[:, first : first + size])
        xb[0:64, to], xb[64:128, to], xb[128:192, to], xb[192:256, to] = hi, lo, hi, lo

    def multiply(rel, part):
        w = wts[rel * NK * 16 : (rel + 1) * NK * 16, :]
        for t in range(SPAN // 256):
            first = part * HALF + t * 256
            big[:, t * 256 : (t + 1) * 256] = jnp.dot(
                w, xb[:, first : first + 256], preferred_element_type=F32
            )

    def partial_rows(half):
        acc = jnp.zeros((8, HALF), F32)
        for k in range(NK):
            g = big[k * 16 + half * 8 : k * 16 + half * 8 + 8, :]
            acc = acc + pltpu.roll(g, (k - KB) % SPAN, 1)[:, 128 : 128 + HALF]
        return acc

    for part in range(2):
        load_bins(part)
        multiply(0, part)
        for half in range(2):
            psend[part, half] = partial_rows(half)
            pair = pltpu.make_async_remote_copy(
                src_ref=psend.at[part, half],
                dst_ref=precv.at[part, half],
                send_sem=psem_s.at[part, half],
                recv_sem=psem_r.at[part, half],
                device_id={"grp": grp ^ 1},
                device_id_type=MESH,
            )
            pair.start()
            pairs.append(pair)
        multiply(1, part)
        for half in range(2):
            tile = partial_rows(half)
            pairs[2 * part + half].wait_recv()
            tile = tile + precv[part, half]
            rsend[part, 2 * half] = tile[0:4]
            rsend[part, 2 * half + 1] = tile[4:8]
            for q in (2 * half, 2 * half + 1):
                mine = (zh == goal) & (zl == q)

                @pl.when(mine)
                def _():
                    pltpu.make_async_copy(
                        rsend.at[part, q], rrecv.at[part, zh], rsem_r.at[part, zh]
                    ).start()

                @pl.when(jnp.logical_not(mine))
                def _():
                    pltpu.make_async_remote_copy(
                        src_ref=rsend.at[part, q],
                        dst_ref=rrecv.at[part, zh],
                        send_sem=rsem_s.at[part, q],
                        recv_sem=rsem_r.at[part, zh],
                        device_id=device(x, goal, y, q, c),
                        device_id_type=MESH,
                    ).start()

    b, shared = [], []
    for part in range(2):
        half1 = base_rows(0, part)
        for q in range(4):
            piece = rrecv.at[part, q]
            pltpu.make_async_copy(piece, piece, rsem_r.at[part, q]).wait()
        b.append((rrecv[part, 0] + rrecv[part, 1]) + (rrecv[part, 2] + rrecv[part, 3]))
        shared += share(0, part, part * HALF, half1 + b[part])
    v1 = smooth(0, shared, sent_w)
    pad_columns(v1)

    sent_w = spread(wsem_s.at[1], wsem_r.at[1], window, lambda g: win.at[1, g])
    sent_q = sent_q + base(1)
    sent = pairs + shared + sent_w + sent_q
    half2 = [base_rows(1, part) + b[part] for part in range(2)]
    shared = share(1, 0, 0, jnp.concatenate(half2, axis=1))
    for part in range(2):
        given(part, asem_s)
        for q in range(4):

            @pl.when(jnp.logical_not((zh == goal) & (zl == q)))
            def _():
                piece = rsend.at[part, q]
                pltpu.make_async_copy(piece, piece, rsem_s.at[part, q]).wait()

    out[0] = smooth(1, shared, sent)
    for copy in shared:
        copy.wait_send()


def on_device(measured, drift, start_volume):
    scale, slots, t4, f_hi, b_hi = tables()
    vmem = pl.BlockSpec(memory_space=pltpu.VMEM)
    hbm = pl.BlockSpec(memory_space=pltpu.HBM)
    dma = pltpu.SemaphoreType.DMA
    scratch = [
        pltpu.VMEM(t4.shape, BF16),
        pltpu.VMEM(f_hi.shape, BF16),
        pltpu.VMEM(b_hi.shape, BF16),
        pltpu.VMEM((64, C), F32),
        pltpu.VMEM((8, C), F32),
        pltpu.VMEM((2 * NK * 16, 256), BF16),
        pltpu.VMEM((256, WIDE), BF16),
        pltpu.VMEM((NK * 16, SPAN), F32),
        pltpu.VMEM((2, 2, 8, HALF), F32),
        pltpu.VMEM((2, 2, 8, HALF), F32),
        pltpu.VMEM((2, 4, 4, HALF), F32),
        pltpu.VMEM((2, 4, 4, HALF), F32),
        pltpu.VMEM((4, C + 128), F32),
        pltpu.VMEM((2, 8, 4, WIN), F32),
        pltpu.VMEM((128, WIN), BF16),
        pltpu.VMEM((NJ * NR, WIN), F32),
        pltpu.VMEM((NKP * NR, 256), BF16),
        pltpu.VMEM((A, 128), F32),
        pltpu.VMEM((A, 256), BF16),
        pltpu.VMEM((2, 8, 4, OWN), F32),
        pltpu.VMEM((2, 4, C), F32),
        pltpu.VMEM((2, 4, C), F32),
        pltpu.VMEM((2, 2, 4, C), F32),
        pltpu.VMEM((2, 4, C), F32),
        dma((3,)),
        dma((2,)),
        dma((2,)),
        dma((2, 2)),
        dma((2, 2)),
        dma((2, 4)),
        dma((2, 4)),
        dma((2, 8)),
        dma((2, 8)),
        dma((2, 8)),
        dma((2, 8)),
        dma((2, 2, 6)),
        dma((2, 2, 6)),
    ]
    return pl.pallas_call(
        functools.partial(kernel, float(scale)),
        out_shape=jax.ShapeDtypeStruct(start_volume.shape, F32),
        in_specs=[hbm, vmem, vmem, vmem] + [hbm] * 3,
        out_specs=vmem,
        scratch_shapes=scratch,
        compiler_params=pltpu.CompilerParams(
            collective_id=0, has_side_effects=True, vmem_limit_bytes=2**26 - 2**18
        ),
        name="sirt",
    )(
        measured,
        drift.reshape(4, 128),
        start_volume,
        jnp.asarray(slots),
        *(jnp.asarray(t) for t in (t4, f_hi, b_hi)),
    )


def solution(mesh):
    in_specs = (P(("wide", "grp"), None, None), P(), P("wide", "grp", None))
    return jax.shard_map(
        on_device, mesh=mesh, in_specs=in_specs, out_specs=P("wide", "grp", None), check_vma=False
    )
```
